32 devices in a mesh: rows: 4 (over x, core), seq: 8 (over z, y).
Axes of the slice: x: 2, y: 2, z: 4, core: 2. Of those that a mesh axis runs over, the one named last changes fastest.
Arguments:
- target: bfloat16 [8, 2048, 768], P('rows', 'seq'), may hold values from -6 to 6
- memory: bfloat16 [8, 2048, 768], P('rows', 'seq'), may hold values from -6 to 6
- target_seg: int32 [8, 2048], P('rows', 'seq'), may hold values from 0 to 2, as said below
- memory_seg: int32 [8, 2048], P('rows', 'seq'), may hold values from 0 to 2, as said below
- grad_output: bfloat16 [8, 2048, 768], P('rows', 'seq'), may hold values from -6 to 6
- self_query: float32 [768, 768], P(('rows', 'seq')), may hold values from -0.21875 to 0.21875
- self_qbias: float32 [768], P(('rows', 'seq')), may hold values from -3 to 3
- self_key: float32 [768, 768], P(('rows', 'seq')), may hold values from -0.21875 to 0.21875
- self_value: float32 [768, 768], P(('rows', 'seq')), may hold values from -0.21875 to 0.21875
- self_vbias: float32 [768], P(('rows', 'seq')), may hold values from -3 to 3
- self_out: float32 [768, 768], P(('rows', 'seq')), may hold values from -1.75 to 1.75
- self_obias: float32 [768], P(('rows', 'seq')), may hold values from -3 to 3
- norm1_gain: float32 [768], P(('rows', 'seq')), may hold values from 0.25 to 1.75
- norm1_shift: float32 [768], P(('rows', 'seq')), may hold values from -3 to 3
- cross_query: float32 [768, 768], P(('rows', 'seq')), may hold values from -0.21875 to 0.21875
- cross_qbias: float32 [768], P(('rows', 'seq')), may hold values from -3 to 3
- cross_key: float32 [768, 768], P(('rows', 'seq')), may hold values from -0.21875 to 0.21875
- cross_value: float32 [768, 768], P(('rows', 'seq')), may hold values from -0.21875 to 0.21875
- cross_vbias: float32 [768], P(('rows', 'seq')), may hold values from -3 to 3
- cross_out: float32 [768, 768], P(('rows', 'seq')), may hold values from -1.75 to 1.75
- cross_obias: float32 [768], P(('rows', 'seq')), may hold values from -3 to 3
- norm2_gain: float32 [768], P(('rows', 'seq')), may hold values from 0.25 to 1.75
- norm2_shift: float32 [768], P(('rows', 'seq')), may hold values from -3 to 3
- ffn_up: float32 [768, 3072], P(('rows', 'seq')), may hold values from -0.21875 to 0.21875
- ffn_ubias: float32 [3072], P(('rows', 'seq')), may hold values from -3 to 3
- ffn_down: float32 [3072, 768], P(('rows', 'seq')), may hold values from -0.21875 to 0.21875
- ffn_dbias: float32 [768], P(('rows', 'seq')), may hold values from -3 to 3
- norm3_gain: float32 [768], P(('rows', 'seq')), may hold values from 0.25 to 1.75
- norm3_shift: float32 [768], P(('rows', 'seq')), may hold values from -3 to 3
Outputs:
- output: bfloat16 [8, 2048, 768], P('rows', 'seq')
- target_gradient: bfloat16 [8, 2048, 768], P('rows', 'seq')
- memory_gradient: bfloat16 [8, 2048, 768], P('rows', 'seq')
- self_query_gradient: float32 [768, 768], P(('rows', 'seq'))
- self_query_bias_gradient: float32 [768], P(('rows', 'seq'))
- self_key_gradient: float32 [768, 768], P(('rows', 'seq'))
- self_value_gradient: float32 [768, 768], P(('rows', 'seq'))
- self_value_bias_gradient: float32 [768], P(('rows', 'seq'))
- self_output_gradient: float32 [768, 768], P(('rows', 'seq'))
- self_output_bias_gradient: float32 [768], P(('rows', 'seq'))
- first_gain_gradient: float32 [768], P(('rows', 'seq'))
- first_shift_gradient: float32 [768], P(('rows', 'seq'))
- cross_query_gradient: float32 [768, 768], P(('rows', 'seq'))
- cross_query_bias_gradient: float32 [768], P(('rows', 'seq'))
- cross_key_grad_array: float32 [768, 768], P(('rows', 'seq'))
- cross_value_grad_array: float32 [768, 768], P(('rows', 'seq'))
- cross_value_bias_gradient: float32 [768], P(('rows', 'seq'))
- cross_output_gradient: float32 [768, 768], P(('rows', 'seq'))
- cross_output_bias_gradient: float32 [768], P(('rows', 'seq'))
- second_gain_gradient: float32 [768], P(('rows', 'seq'))
- second_shift_gradient: float32 [768], P(('rows', 'seq'))
- up_weight_gradient: float32 [768, 3072], P(('rows', 'seq'))
- up_bias_gradient: float32 [3072], P(('rows', 'seq'))
- down_weight_gradient: float32 [3072, 768], P(('rows', 'seq'))
- down_bias_gradient: float32 [768], P(('rows', 'seq'))
- third_gain_gradient: float32 [768], P(('rows', 'seq'))
- third_shift_gradient: float32 [768], P(('rows', 'seq'))
The draws below stay inside these ranges and needn't reach their ends.
Inputs may be any that keep to these rules, and one draw needn't show every extreme that they name: `target_seg`: in every row the ids never fall and take each of 0, 1 and 2; id 0 holds the first 1 to 255 positions and id 2 the last 1 to 255. `memory_seg`: in every row the ids never fall and take each of 0, 1 and 2; id 0 holds the first 1 to 255 positions and id 2 the last 1 to 255.
All inputs are finite; a program needn't handle non-finite values.
Results may differ from the reference program's by a relative error of at most 0.024.
The reference program's roundings to bfloat16 on the way count: a program that leaves them out, or rounds other values in their place, can miss the bound.
Values may be sent and summed in bfloat16 or wider, within the bound.
A program may use at most 192 MiB of HBM per device.

```python
import jax
import jax.numpy as jnp
from jax import lax

D = 768
FF = 3072
HEADS = 12
HEAD_DIM = 64
LENGTH = 2048
MEM_LEN = 2048
ROWS = 8
SHARD = 256
MEM_SHARD = 256


def segment_ids(key, count, length, shard):
    first = jax.random.randint(jax.random.fold_in(key, 1), (count, 1), 1, shard)
    tail = jax.random.randint(jax.random.fold_in(key, 2), (count, 1), 1, shard)
    places = jnp.arange(length, dtype=jnp.int32)[None, :]
    return (places >= first).astype(jnp.int32) + (places >= length - tail).astype(jnp.int32)


def draw_target_seg(key, part):
    return segment_ids(jax.random.fold_in(key, 11), ROWS, LENGTH, SHARD)


def draw_memory_seg(key, part):
    return segment_ids(jax.random.fold_in(key, 12), ROWS, MEM_LEN, MEM_SHARD)


def block_scale(key, extent, pieces, smallest, top_value):
    level, own = 1.0, jax.random.fold_in(key, 6)
    for position, shards_of in pieces:
        heights = jnp.exp(jax.random.uniform(jax.random.fold_in(own, position), (shards_of,), jnp.float32, smallest / len(pieces), top_value / len(pieces)))
        level = level * jnp.repeat(heights, extent[position] // shards_of).reshape([-1 if axis == position else 1 for axis in range(len(extent))])
    return level


def scatter_about(own_key, dims, spread, most, pieces=(), kind=jnp.bfloat16):
    factor_of = block_scale(own_key, dims, pieces, -0.22, 0.18) if pieces else 1.0
    drawn = jax.random.normal(own_key, dims, jnp.float32) * spread * factor_of
    return jnp.minimum(jnp.maximum(drawn, -most), most).astype(kind)


def setup_inputs(seed: int = 0) -> dict:
    seeds = jax.random.split(jax.random.key(seed), 30)
    return {
        "target": scatter_about(seeds[0], (ROWS, LENGTH, D), 1.0, 6.0, ((0, 4), (1, 8))),
        "memory": scatter_about(seeds[1], (ROWS, MEM_LEN, D), 1.0, 6.0, ((0, 4), (1, 8))),
        "target_seg": draw_target_seg(jax.random.fold_in(seeds[29], 71), 0),
        "memory_seg": draw_memory_seg(jax.random.fold_in(seeds[29], 71), 0),
        "grad_output": scatter_about(seeds[4], (ROWS, LENGTH, D), 1.0, 6.0, ((0, 4), (1, 8))),
        "self_query": scatter_about(seeds[5], (D, D), D ** -0.5, 0.21875, ((0, 32),), jnp.float32),
        "self_qbias": scatter_about(seeds[6], (D,), 0.5, 3.0, ((0, 32),), jnp.float32),
        "self_key": scatter_about(seeds[7], (D, D), D ** -0.5, 0.21875, ((0, 32),), jnp.float32),
        "self_value": scatter_about(seeds[8], (D, D), D ** -0.5, 0.21875, ((0, 32),), jnp.float32),
        "self_vbias": scatter_about(seeds[9], (D,), 0.5, 3.0, ((0, 32),), jnp.float32),
        "self_out": scatter_about(seeds[10], (D, D), (D // 64) ** -0.5, 1.75, ((0, 32),), jnp.float32),
        "self_obias": scatter_about(seeds[11], (D,), 0.5, 3.0, ((0, 32),), jnp.float32),
        "norm1_gain": jnp.clip(1.0 + 0.15 * jax.random.normal(seeds[12], (D,), jnp.float32), 0.25, 1.75),
        "norm1_shift": scatter_about(seeds[13], (D,), 0.5, 3.0, ((0, 32),), jnp.float32),
        "cross_query": scatter_about(seeds[14], (D, D), D ** -0.5, 0.21875, ((0, 32),), jnp.float32),
        "cross_qbias": scatter_about(seeds[15], (D,), 0.5, 3.0, ((0, 32),), jnp.float32),
        "cross_key": scatter_about(seeds[16], (D, D), D ** -0.5, 0.21875, ((0, 32),), jnp.float32),
        "cross_value": scatter_about(seeds[17], (D, D), D ** -0.5, 0.21875, ((0, 32),), jnp.float32),
        "cross_vbias": scatter_about(seeds[18], (D,), 0.5, 3.0, ((0, 32),), jnp.float32),
        "cross_out": scatter_about(seeds[19], (D, D), (D // 64) ** -0.5, 1.75, ((0, 32),), jnp.float32),
        "cross_obias": scatter_about(seeds[20], (D,), 0.5, 3.0, ((0, 32),), jnp.float32),
        "norm2_gain": jnp.clip(1.0 + 0.15 * jax.random.normal(seeds[21], (D,), jnp.float32), 0.25, 1.75),
        "norm2_shift": scatter_about(seeds[22], (D,), 0.5, 3.0, ((0, 32),), jnp.float32),
        "ffn_up": scatter_about(seeds[23], (D, FF), D ** -0.5, 0.21875, ((0, 32),), jnp.float32),
        "ffn_ubias": scatter_about(seeds[24], (FF,), 0.5, 3.0, ((0, 32),), jnp.float32),
        "ffn_down": scatter_about(seeds[25], (FF, D), (FF // 4) ** -0.5, 0.21875, ((0, 32),), jnp.float32),
        "ffn_dbias": scatter_about(seeds[26], (D,), 0.5, 3.0, ((0, 32),), jnp.float32),
        "norm3_gain": jnp.clip(1.0 + 0.15 * jax.random.normal(seeds[27], (D,), jnp.float32), 0.25, 1.75),
        "norm3_shift": scatter_about(seeds[28], (D,), 0.5, 3.0, ((0, 32),), jnp.float32),
    }


epsilon = 1e-05
big_negative = -1e+30
score_scale = 0.125
highest = lax.Precision.HIGHEST

@jax.custom_vjp
def lower_precision(v):
    return lax.optimization_barrier(v.astype(jnp.bfloat16)).astype(jnp.float32)

@jax.custom_vjp
def lower_precision_backward(v):
    return v

def low_keep(v):
    return (lower_precision(v), None)

def low_pass(kept, grad):
    return (grad,)

def back_keep(v):
    return (v, None)

def back_low(kept, grad):
    return (lower_precision(grad),)
lower_precision.defvjp(low_keep, low_pass)
lower_precision_backward.defvjp(back_keep, back_low)

def matrix_multiply(left, right):
    return jnp.dot(left, right, precision=highest)

def layer_norm(resid, gain, shift):
    mean = lax.optimization_barrier(jnp.mean(resid, axis=-1, keepdims=True))
    centered = resid - mean
    variance = lax.optimization_barrier(jnp.mean(centered * centered, axis=-1, keepdims=True))
    return centered * lax.rsqrt(variance + epsilon) * gain + shift

def attention(queries, keys, values, query_seg, key_seg, causal):
    length = queries.shape[0]
    span = 512 if length % 512 == 0 else length
    blocks = length // span
    query_heads = queries.reshape(blocks, span, HEADS, HEAD_DIM)
    query_segs = query_seg.reshape(blocks, span)
    query_pos = jnp.arange(length, dtype=jnp.int32).reshape(blocks, span)
    key_heads = keys.reshape(keys.shape[0], HEADS, HEAD_DIM)
    value_heads = values.reshape(values.shape[0], HEADS, HEAD_DIM)
    key_pos = jnp.arange(keys.shape[0], dtype=jnp.int32)

    @jax.checkpoint
    def one_block(block):
        heads, segs, places = block
        scores = lower_precision_backward(jnp.einsum('qhd,khd->hqk', heads, key_heads, precision=highest) * score_scale)
        allowed = segs[:, None] == key_seg[None, :]
        if causal:
            allowed = jnp.logical_and(allowed, key_pos[None, :] <= places[:, None])
        masked = jnp.where(allowed[None], scores, big_negative)
        top = lax.optimization_barrier(jnp.max(masked, axis=-1, keepdims=True))
        raised = jnp.exp(masked - top)
        shares = raised / lax.optimization_barrier(jnp.sum(raised, axis=-1, keepdims=True))
        return jnp.einsum('hqk,khd->qhd', shares, value_heads, precision=highest)
    return lax.map(one_block, (query_heads, query_segs, query_pos)).reshape(length, HEADS * HEAD_DIM)

def decoder(weight_list, target, memory, target_seg, memory_seg):
    query_matrix, query_vector, key_matrix, value_matrix, value_vector, output_matrix, output_vector, first_gain, first_shift, cross_query_matrix, cross_query_vector, cross_key_matrix, cross_value_matrix, cross_value_vector, cross_output_matrix, cross_output_vector, second_gain, second_shift, up_matrix, up_vector, down_matrix, down_vector, third_gain, third_shift = [lower_precision(weight_matrix) for weight_matrix in weight_list]
    queries = lower_precision(lower_precision_backward(matrix_multiply(target, query_matrix) + query_vector))
    keys = lower_precision(lower_precision_backward(matrix_multiply(target, key_matrix)))
    values = lower_precision(lower_precision_backward(matrix_multiply(target, value_matrix) + value_vector))
    self_attn = lower_precision(lower_precision_backward(attention(queries, keys, values, target_seg, target_seg, True)))
    resid_one = target + lower_precision_backward(matrix_multiply(self_attn, output_matrix) + output_vector)
    hidden_one = layer_norm(resid_one, first_gain, first_shift)
    hidden_round = lower_precision(hidden_one)
    cross_queries = lower_precision(lower_precision_backward(matrix_multiply(hidden_round, cross_query_matrix) + cross_query_vector))
    cross_keys = lower_precision(lower_precision_backward(matrix_multiply(memory, cross_key_matrix)))
    cross_value_rows = lower_precision(lower_precision_backward(matrix_multiply(memory, cross_value_matrix) + cross_value_vector))
    cross_attn = lower_precision(lower_precision_backward(attention(cross_queries, cross_keys, cross_value_rows, target_seg, memory_seg, False)))
    resid_two = hidden_one + lower_precision_backward(matrix_multiply(cross_attn, cross_output_matrix) + cross_output_vector)
    hidden_two = layer_norm(resid_two, second_gain, second_shift)
    inner_pre = lower_precision_backward(matrix_multiply(lower_precision(hidden_two), up_matrix) + up_vector)
    active = lower_precision(jax.nn.gelu(inner_pre, approximate=False))
    resid_three = hidden_two + lower_precision_backward(matrix_multiply(active, down_matrix) + down_vector)
    return layer_norm(resid_three, third_gain, third_shift)

def reference(target, memory, target_seg, memory_seg, grad_output, self_query, self_qbias, self_key, self_value, self_vbias, self_out, self_obias, norm1_gain, norm1_shift, cross_query, cross_qbias, cross_key, cross_value, cross_vbias, cross_out, cross_obias, norm2_gain, norm2_shift, ffn_up, ffn_ubias, ffn_down, ffn_dbias, norm3_gain, norm3_shift):
    params = (self_query, self_qbias, self_key, self_value, self_vbias, self_out, self_obias, norm1_gain, norm1_shift, cross_query, cross_qbias, cross_key, cross_value, cross_vbias, cross_out, cross_obias, norm2_gain, norm2_shift, ffn_up, ffn_ubias, ffn_down, ffn_dbias, norm3_gain, norm3_shift)

    def one_row(partial_sums, row):
        target_row, memory_row, tseg_row, mseg_row, cotangent = row

        def forward(weight_list, target_in, memory_in):
            return decoder(weight_list, target_in, memory_in, tseg_row, mseg_row)
        result, pullback = jax.vjp(forward, params, target_row.astype(jnp.float32), memory_row.astype(jnp.float32))
        weight_grads, target_grad, memory_grad = pullback(cotangent.astype(jnp.float32))
        partial_sums = jax.tree.map(lambda total, grad: total + grad, partial_sums, weight_grads)
        return (partial_sums, (result.astype(jnp.bfloat16), target_grad.astype(jnp.bfloat16), memory_grad.astype(jnp.bfloat16)))
    start = jax.tree.map(jnp.zeros_like, params)
    partial_sums, stacked = lax.scan(one_row, start, (target, memory, target_seg, memory_seg, grad_output))
    output, target_gradient, memory_gradient = stacked
    self_query_gradient, self_query_bias_gradient, self_key_gradient, self_value_gradient, self_value_bias_gradient, self_output_gradient, self_output_bias_gradient, first_gain_gradient, first_shift_gradient, cross_query_gradient, cross_query_bias_gradient, cross_key_grad_array, cross_value_grad_array, cross_value_bias_gradient, cross_output_gradient, cross_output_bias_gradient, second_gain_gradient, second_shift_gradient, up_weight_gradient, up_bias_gradient, down_weight_gradient, down_bias_gradient, third_gain_gradient, third_shift_gradient = partial_sums
    return (output, target_gradient, memory_gradient, self_query_gradient, self_query_bias_gradient, self_key_gradient, self_value_gradient, self_value_bias_gradient, self_output_gradient, self_output_bias_gradient, first_gain_gradient, first_shift_gradient, cross_query_gradient, cross_query_bias_gradient, cross_key_grad_array, cross_value_grad_array, cross_value_bias_gradient, cross_output_gradient, cross_output_bias_gradient, second_gain_gradient, second_shift_gradient, up_weight_gradient, up_bias_gradient, down_weight_gradient, down_bias_gradient, third_gain_gradient, third_shift_gradient)
```

```python
import functools

import jax
import jax.numpy as jnp
from jax import lax
from jax.experimental import pallas as pl
from jax.experimental.pallas import tpu as pltpu
from jax.sharding import PartitionSpec as P

f32=jnp.float32; bf16=jnp.bfloat16
NT=(((1,),(1,)),((),()))
TN=(((0,),(0,)),((),()))
def dot(a,b,dims=(((1,),(0,)),((),()))): return lax.dot_general(a,b,dims,preferred_element_type=f32)

def fwd_kernel(causal, chunk, q_ref, kv_ref, kaug_ref, qaug_ref, o_ref, lse_ref):
    p=pl.program_id(1)
    nq=q_ref.shape[1]; nk=kv_ref.shape[1]
    lane=lax.broadcasted_iota(jnp.int32,(nq,128),1)
    q=q_ref[0]*jnp.asarray(0.125,bf16)
    qaug=qaug_ref[0]
    zero=jnp.zeros_like(q)
    outs=[];lses=[]
    for h in range(2):
        mine = (lane<64) if h==0 else (lane>=64)
        qc=jnp.concatenate([jnp.where(mine,q,zero),qaug],axis=1)
        ss=[]; m=None
        for c in range(nk//chunk):
            kc=jnp.concatenate([kv_ref[0,c*chunk:(c+1)*chunk,0:128],kaug_ref[0,c*chunk:(c+1)*chunk,:]],axis=1)
            s=dot(qc,kc,NT)
            if causal and c*chunk<nq:
                ki=c*chunk+lax.broadcasted_iota(jnp.int32,s.shape,1); qi=lax.broadcasted_iota(jnp.int32,s.shape,0)
                s=jnp.where((ki>=nq)|(ki<=qi),s,-1e30)
            ss.append(s)
            mc=jnp.max(s,axis=1,keepdims=True)
            m=mc if m is None else jnp.maximum(m,mc)
        l=None;o=None
        for c in range(nk//chunk):
            e=jnp.exp(ss[c]-m)
            lc=jnp.sum(e,axis=1,keepdims=True)
            oc=dot(e.astype(bf16),kv_ref[0,c*chunk:(c+1)*chunk,128:256])
            l=lc if l is None else l+lc
            o=oc if o is None else o+oc
        outs.append(o/l); lses.append(m+jnp.log(l))
    o_ref[0]=jnp.where(lane<64,outs[0],outs[1])
    @pl.when(p==0)
    def _(): lse_ref[...]=jnp.zeros_like(lse_ref)
    lse_ref[0]=jnp.where(lane==2*p,lses[0],jnp.where(lane==2*p+1,lses[1],lse_ref[0]))

def attn_fwd(q,kv,kaug,qaug,causal,chunk=512):
    R,nq,D=q.shape; nk=kv.shape[1]; npair=D//128
    return pl.pallas_call(functools.partial(fwd_kernel,causal,chunk),
        grid=(R,npair),
        in_specs=[pl.BlockSpec((1,nq,128),lambda b,p:(b,0,p)),
                  pl.BlockSpec((1,nk,256),lambda b,p:(b,0,p)),
                  pl.BlockSpec((1,nk,128),lambda b,p:(b,0,0)),
                  pl.BlockSpec((1,nq,128),lambda b,p:(b,0,0))],
        out_specs=[pl.BlockSpec((1,nq,128),lambda b,p:(b,0,p)),
                   pl.BlockSpec((1,nq,128),lambda b,p:(b,0,0))],
        out_shape=[jax.ShapeDtypeStruct((R,nq,D),f32),jax.ShapeDtypeStruct((R,nq,128),f32)],
        compiler_params=pltpu.CompilerParams(vmem_limit_bytes=40<<20),
        name="attn_fwd")(q,kv,kaug,qaug)

def split3(x):
    a=x.astype(bf16); r=x-a.astype(f32); b=r.astype(bf16); c=(r-b.astype(f32)).astype(bf16)
    return a,b,c

def bwd_kernel(causal, chunk, q_ref, kv_ref, kaug_ref, qaug_ref, lse_ref, o_ref, do_ref, dq_ref, dkv_ref):
    p=pl.program_id(1)
    nq=q_ref.shape[1]; nk=kv_ref.shape[1]
    lane=lax.broadcasted_iota(jnp.int32,(nq,128),1)
    q=q_ref[0]*jnp.asarray(0.125,bf16); do=do_ref[0]
    zero=jnp.zeros_like(q)
    prod=do.astype(f32)*o_ref[0]
    qcs=[];dcs=[];qm=[];dm=[]
    for h in range(2):
        mine = (lane<64) if h==0 else (lane>=64)
        lse=jnp.sum(jnp.where(lane==2*p+h,lse_ref[0],0.0),axis=1,keepdims=True)
        delta=jnp.sum(jnp.where(mine,prod,0.0),axis=1,keepdims=True)
        a,b,c=split3(-lse); d,e,f=split3(-delta)
        aug=jnp.where(lane==8,a,jnp.where(lane==9,b,jnp.where(lane==10,c,qaug_ref[0])))
        daug=jnp.where(lane==8,d,jnp.where(lane==9,e,jnp.where(lane==10,f,zero)))
        qm.append(jnp.where(mine,q,zero)); dm.append(jnp.where(mine,do,zero))
        qcs.append(jnp.concatenate([qm[h],aug],axis=1)); dcs.append(jnp.concatenate([dm[h],daug],axis=1))
    qq=jnp.concatenate(qm,axis=0); dd=jnp.concatenate(dm,axis=0)
    dq=[None,None]
    for c in range(nk//chunk):
        sl=slice(c*chunk,(c+1)*chunk)
        k=kv_ref[0,sl,0:128]; v=kv_ref[0,sl,128:256]; ka=kaug_ref[0,sl,:]
        kc=jnp.concatenate([k,ka],axis=1); vc=jnp.concatenate([v,ka],axis=1)
        pts=[];dss=[]
        for h in range(2):
            st=dot(kc,qcs[h],NT)
            if causal and c*chunk<nq:
                ki=c*chunk+lax.broadcasted_iota(jnp.int32,st.shape,0); qi=lax.broadcasted_iota(jnp.int32,st.shape,1)
                st=jnp.where((ki>=nq)|(ki<=qi),st,-1e30)
            pt=jnp.exp(st)
            ds=(pt*dot(vc,dcs[h],NT)).astype(bf16)
            pts.append(pt.astype(bf16)); dss.append(ds)
            g=dot(ds,k,TN)
            dq[h]=g if dq[h] is None else dq[h]+g
        dk=dot(jnp.concatenate(dss,axis=1),qq)
        dv=dot(jnp.concatenate(pts,axis=1),dd)
        dkv_ref[0,sl,0:128]=dk.astype(bf16)
        dkv_ref[0,sl,128:256]=dv.astype(bf16)
    dq_ref[0]=(jnp.where(lane<64,dq[0],dq[1])*0.125).astype(bf16)

def attn_bwd(q,kv,kaug,qaug,lse,o,do,causal,chunk=2048):
    R,nq,D=q.shape; nk=kv.shape[1]; npair=D//128
    qs=pl.BlockSpec((1,nq,128),lambda b,p:(b,0,p)); q0=pl.BlockSpec((1,nq,128),lambda b,p:(b,0,0))
    return pl.pallas_call(functools.partial(bwd_kernel,causal,chunk),
        grid=(R,npair),
        in_specs=[qs,pl.BlockSpec((1,nk,256),lambda b,p:(b,0,p)),pl.BlockSpec((1,nk,128),lambda b,p:(b,0,0)),q0,q0,qs,qs],
        out_specs=[qs,pl.BlockSpec((1,nk,256),lambda b,p:(b,0,p))],
        out_shape=[jax.ShapeDtypeStruct((R,nq,D),bf16),jax.ShapeDtypeStruct((R,nk,2*D),bf16)],
        compiler_params=pltpu.CompilerParams(vmem_limit_bytes=40<<20),
        name="attn_bwd")(q,kv,kaug,qaug,lse,o,do)


HEADS = 12
EPS = 1e-05
BIG = -1e30
BOTH = ("rows", "seq")


def ring_order(n):
    ny = 2 ** ((n.bit_length() - 1) // 2)
    nz = n // ny
    if ny < 2 or nz < 2:
        return list(range(n))
    order = []
    for z in range(nz):
        ys = list(range(1, ny)) if z % 2 == 0 else list(range(ny - 1, 0, -1))
        order += [z * ny + y for y in ys]
    order += [z * ny for z in range(nz - 1, -1, -1)]
    return order


class Ring:
    def __init__(self, n):
        self.n = n
        self.order = ring_order(n)
        self.up = [(self.order[i], self.order[(i + 1) % n]) for i in range(n)]
        self.down = [(b, a) for a, b in self.up]
        self.near = (n - 1) // 2
        self.far = n - 1 - self.near
        self.offsets = [0]
        for d in range(1, self.far + 1):
            self.offsets.append(-d)
            if d <= self.near:
                self.offsets.append(d)
        place = [0] * n
        for i, s in enumerate(self.order):
            place[s] = i
        me = lax.axis_index("seq")
        every = jnp.arange(n, dtype=jnp.int32)
        spot = jnp.sum(jnp.where(every == me, jnp.asarray(place, jnp.int32), 0))
        at = (spot + jnp.asarray(self.offsets, jnp.int32) + n) % n
        self.owners = jnp.sum(jnp.where(at[:, None] == every, jnp.asarray(self.order, jnp.int32), 0), axis=1)

    def arrange(self, x):
        pick = (self.owners[:, None] == jnp.arange(self.n)).reshape((self.n, self.n) + (1,) * (x.ndim - 1))
        return jnp.sum(jnp.where(pick, x[None], 0), axis=1)

    def gather(self, x):
        low, high = x, x
        parts = {0: x}
        for d in range(1, self.far + 1):
            low = lax.ppermute(low, "seq", self.up)
            parts[-d] = low
            if d <= self.near:
                high = lax.ppermute(high, "seq", self.down)
                parts[d] = high
        return [parts[o] for o in self.offsets]

    def reduce(self, pieces):
        part = dict(zip(self.offsets, pieces))
        total = part[0].astype(f32)
        for sign, count, perm in ((-1, self.far, self.down), (1, self.near, self.up)):
            if count == 0:
                continue
            acc = part[sign * count]
            for d in range(count - 1, 0, -1):
                acc = lax.ppermute(acc, "seq", perm)
                acc = (acc.astype(f32) + part[sign * d].astype(f32)).astype(bf16)
            total = total + lax.ppermute(acc, "seq", perm).astype(f32)
        return total


def halve(x, rows, seq):
    rest = x.shape[1:]
    dims = []
    for axis, n in (("rows", rows), ("seq", seq)):
        bits = n.bit_length() - 1
        for b in range(bits - 1, -1, -1):
            dims.append((axis, n, b))
    x = x.reshape((2,) * len(dims) + rest)
    order = sorted(range(len(dims)), key=lambda i: (dims[i][0] != "rows", dims[i][2]))
    left = list(range(len(dims)))
    for i in order:
        axis, n, b = dims[i]
        at = left.index(i)
        mine = (lax.axis_index(axis) >> b) & 1
        keep = lax.dynamic_index_in_dim(x, mine, at, keepdims=False)
        send = lax.dynamic_index_in_dim(x, 1 - mine, at, keepdims=False)
        got = lax.ppermute(send, axis, [(j, j ^ (1 << b)) for j in range(n)])
        x = (keep.astype(f32) + got.astype(f32)).astype(bf16)
        left.remove(i)
    return x


def norm(resid, gain, shift):
    mean = jnp.mean(resid, axis=-1, keepdims=True)
    centered = resid - mean
    inv = lax.rsqrt(jnp.mean(centered * centered, axis=-1, keepdims=True) + EPS)
    unit = centered * inv
    return unit * gain + shift, unit, inv


def norm_back(dy, unit, inv, gain):
    f = dy * gain
    mean = jnp.mean(f, axis=-1, keepdims=True)
    cross = jnp.mean(f * unit, axis=-1, keepdims=True)
    return (f - mean - unit * cross) * inv, jnp.sum(dy * unit, axis=0), jnp.sum(dy, axis=0)


def colsum(x):
    return jnp.sum(x.astype(f32), axis=0)


def key_marks(seg, hidden):
    lane = jnp.arange(128)
    marks = jnp.where(lane < 3, jnp.where(seg[..., None] == lane, 0.0, BIG), 0.0)
    if hidden is not None:
        marks = jnp.where(lane == 3, jnp.where(hidden[..., None], BIG, 0.0), marks)
    return jnp.where((lane >= 8) & (lane <= 10), 1.0, marks).astype(bf16)


def query_marks(seg):
    lane = jnp.arange(128)
    return ((seg[..., None] == lane) | (lane == 3)).astype(bf16)


def pair_up(a, b):
    lead = a.shape[:-1]
    return jnp.stack([a.reshape(lead + (-1, 128)), b.reshape(lead + (-1, 128))], axis=-2).reshape(lead + (-1,))


def unpair(x):
    y = x.reshape(x.shape[0], -1, 2, 128)
    return y[:, :, 0].reshape(x.shape[0], -1), y[:, :, 1].reshape(x.shape[0], -1)


def layer(nrows, nseq, *args):
    (
        target, memory, target_seg, memory_seg, grad_output,
        self_query, self_qbias, self_key, self_value, self_vbias, self_out, self_obias, norm1_gain, norm1_shift,
        cross_query, cross_qbias, cross_key, cross_value, cross_vbias, cross_out, cross_obias, norm2_gain, norm2_shift,
        ffn_up, ffn_ubias, ffn_down, ffn_dbias, norm3_gain, norm3_shift,
    ) = args
    n = nrows * nseq
    R, L, D = target.shape
    c = self_query.shape[0]
    F = ffn_up.shape[1]
    m = F // D
    ring = Ring(nseq)

    mats = (self_query, self_key, self_value, self_out, cross_query, cross_key, cross_value, cross_out)
    vecs = (
        self_qbias, self_vbias, self_obias, norm1_gain, norm1_shift, cross_qbias, cross_vbias, cross_obias,
        norm2_gain, norm2_shift, ffn_dbias, norm3_gain, norm3_shift, ffn_ubias,
    )
    line = jnp.concatenate([v.astype(bf16) for v in vecs])
    line = jnp.pad(line, (0, 8 * D - line.shape[0])).reshape(8, D)
    pack_a = jnp.concatenate([w.astype(bf16) for w in mats] + [line], axis=0)
    up_rows = ffn_up.astype(bf16).reshape(c, m, D).transpose(1, 0, 2).reshape(m * c, D)
    pack_f = jnp.concatenate([up_rows, ffn_down.astype(bf16)], axis=0)
    all_a = lax.all_gather(pack_a, BOTH, axis=0, tiled=False)
    all_f = lax.all_gather(pack_f, BOTH, axis=0, tiled=False)
    wq, wk, wv, wo, cq, ck, cv, co = [all_a[:, i * c : (i + 1) * c].reshape(D, D) for i in range(8)]
    flat = all_a[:, 8 * c :].reshape(n, -1)
    bq, bv, bo, g1, s1, bcq, bcv, bco, g2, s2, bd, g3, s3 = [
        flat[:, i * c : (i + 1) * c].reshape(D).astype(f32) for i in range(13)
    ]
    bu = flat[:, 13 * c : (13 + m) * c].reshape(F).astype(f32)
    wup = all_f[:, : m * c].reshape(n, m, c, D).transpose(0, 2, 1, 3).reshape(D, F)
    wdown = all_f[:, m * c :].reshape(F, D)

    segs = lax.all_gather(jnp.concatenate([target_seg, memory_seg], axis=0), "seq", axis=0, tiled=False)
    segs = ring.arrange(segs).transpose(1, 0, 2).reshape(2 * R, nseq * L)
    hidden = jnp.repeat(ring.owners > lax.axis_index("seq"), L)[None]
    self_marks = key_marks(segs[:R], hidden)
    cross_marks = key_marks(segs[R:], None)
    marks = query_marks(target_seg)

    X = jnp.stack(ring.gather(target), axis=1).reshape(R * nseq * L, D)
    M = jnp.stack(ring.gather(memory), axis=1).reshape(R * nseq * L, D)
    x = target.reshape(R * L, D)
    wkv, ckv = pair_up(wk, wv), pair_up(ck, cv)
    bkv = pair_up(jnp.zeros_like(bv), bv)
    bckv = pair_up(jnp.zeros_like(bcv), bcv)

    def rows(t):
        return t.reshape(R, -1, t.shape[-1])

    KV = rows((dot(X, wkv) + bkv).astype(bf16))
    Q = rows((dot(x, wq) + bq).astype(bf16))
    A1, lse1 = attn_fwd(Q, KV, self_marks, marks, True)
    a1 = A1.reshape(R * L, D).astype(bf16)
    R1 = x.astype(f32) + dot(a1, wo) + bo
    H1, N1, i1 = norm(R1, g1, s1)
    h1 = H1.astype(bf16)
    CKV = rows((dot(M, ckv) + bckv).astype(bf16))
    CQ = rows((dot(h1, cq) + bcq).astype(bf16))
    A2, lse2 = attn_fwd(CQ, CKV, cross_marks, marks, False)
    a2 = A2.reshape(R * L, D).astype(bf16)
    R2 = H1 + dot(a2, co) + bco
    H2, N2, i2 = norm(R2, g2, s2)
    h2 = H2.astype(bf16)
    U = dot(h2, wup) + bu
    G, gelu_back = jax.vjp(lambda u: jax.nn.gelu(u, approximate=False), U)
    G = G.astype(bf16)
    R3 = H2 + dot(G, wdown) + bd
    out, N3, i3 = norm(R3, g3, s3)
    output = rows(out.astype(bf16))

    dR3, dg3, ds3 = norm_back(grad_output.reshape(R * L, D).astype(f32), N3, i3, g3)
    dZ = dR3.astype(bf16)
    w_down = dot(G, dZ, TN)
    dU = gelu_back(dot(dZ, wdown, NT))[0].astype(bf16)
    w_up = dot(h2, dU, TN)
    up_part = w_up.astype(bf16).reshape(n, c, m, D).transpose(0, 2, 1, 3).reshape(n, m * c, D)
    ffn_part = jnp.concatenate([up_part, w_down.astype(bf16).reshape(n, m * c, D)], axis=1)
    ffn_own = halve(ffn_part, nrows, nseq)
    dH2 = dR3 + dot(dU, wup, NT)
    dR2, dg2, ds2 = norm_back(dH2, N2, i2, g2)
    dO2 = dR2.astype(bf16)
    w_co = dot(a2, dO2, TN)
    dA2 = dot(dO2, co, NT).astype(bf16)
    dCQ, dCKV = attn_bwd(CQ, CKV, cross_marks, marks, lse2, A2, rows(dA2), False)
    dCQ, dCKV = dCQ.reshape(R * L, D), dCKV.reshape(R * nseq * L, 2 * D)
    dH1 = dR2 + dot(dCQ, cq, NT)
    dM = dot(dCKV, ckv, NT).astype(bf16).reshape(R, nseq, L, D)
    memory_gradient = ring.reduce([dM[:, j] for j in range(nseq)]).astype(bf16)
    w_cq = dot(h1, dCQ, TN)
    w_ck, w_cv = unpair(dot(M, dCKV, TN).astype(bf16))
    cross_part = jnp.concatenate(
        [w.astype(bf16).reshape(n, c, D) for w in (w_cq, w_ck, w_cv, w_co)], axis=1
    )
    cross_own = halve(cross_part, nrows, nseq)
    dR1, dg1, ds1 = norm_back(dH1, N1, i1, g1)
    dO1 = dR1.astype(bf16)
    w_o = dot(a1, dO1, TN)
    dA1 = dot(dO1, wo, NT).astype(bf16)
    dQ, dKV = attn_bwd(Q, KV, self_marks, marks, lse1, A1, rows(dA1), True)
    dQ, dKV = dQ.reshape(R * L, D), dKV.reshape(R * nseq * L, 2 * D)
    dX = dot(dKV, wkv, NT).astype(bf16).reshape(R, nseq, L, D)
    far = ring.reduce([dX[:, j] for j in range(nseq)])
    target_gradient = (rows(dR1 + dot(dQ, wq, NT)) + far).astype(bf16)
    w_q = dot(x, dQ, TN)
    w_k, w_v = unpair(dot(X, dKV, TN).astype(bf16))
    sums = (
        colsum(dQ), colsum(dA1), colsum(dO1), dg1, ds1, colsum(dCQ), colsum(dA2), colsum(dO2),
        dg2, ds2, colsum(dZ), dg3, ds3, colsum(dU),
    )
    tail = jnp.concatenate([v.reshape(n, -1) for v in sums], axis=1).astype(bf16)
    tail = jnp.pad(tail, ((0, 0), (0, 8 * D - tail.shape[1]))).reshape(n, 8, D)
    self_part = jnp.concatenate(
        [w.astype(bf16).reshape(n, c, D) for w in (w_q, w_k, w_v, w_o)] + [tail], axis=1
    )
    self_own = halve(self_part, nrows, nseq)

    grads = [self_own[i * c : (i + 1) * c].astype(f32) for i in range(4)]
    grads += [cross_own[i * c : (i + 1) * c].astype(f32) for i in range(4)]
    own = self_own[4 * c :].reshape(-1).astype(f32)
    small = [own[i * c : (i + 1) * c] for i in range(13)] + [own[13 * c : (13 + m) * c]]
    g_up = ffn_own[: m * c].reshape(m, c, D).transpose(1, 0, 2).reshape(c, F).astype(f32)
    g_down = ffn_own[m * c :].astype(f32)
    gq, gk, gv, go, gcq, gck, gcv, gco = grads
    (gbq, gbv, gbo, gg1, gs1, gbcq, gbcv, gbco, gg2, gs2, gbd, gg3, gs3, gbu) = small
    return (
        output, target_gradient, memory_gradient,
        gq, gbq, gk, gv, gbv, go, gbo, gg1, gs1,
        gcq, gbcq, gck, gcv, gbcv, gco, gbco, gg2, gs2,
        g_up, gbu, g_down, gbd, gg3, gs3,
    )


def solution(mesh):
    act, ids, mat, vec = P("rows", "seq", None), P("rows", "seq"), P(BOTH, None), P(BOTH)
    ins = (
        act, act, ids, ids, act,
        mat, vec, mat, mat, vec, mat, vec, vec, vec,
        mat, vec, mat, mat, vec, mat, vec, vec, vec,
        mat, vec, mat, vec, vec, vec,
    )
    outs = (
        act, act, act,
        mat, vec, mat, mat, vec, mat, vec, vec, vec,
        mat, vec, mat, mat, vec, mat, vec, vec, vec,
        mat, vec, mat, vec, vec, vec,
    )
    run = functools.partial(layer, mesh.shape["rows"], mesh.shape["seq"])
    return jax.shard_map(run, mesh=mesh, in_specs=ins, out_specs=outs, check_vma=False)
```

```python
import functools

import jax
import jax.numpy as jnp
from jax import lax
from jax.experimental import pallas as pl
from jax.experimental.pallas import tpu as pltpu
from jax.experimental.layout import Layout, with_layout_constraint
from jax.sharding import PartitionSpec as P

f32 = jnp.float32
bf16 = jnp.bfloat16
EPS = 1e-05
BIG = -1e30
NT = (((1,), (1,)), ((), ()))
TN = (((0,), (0,)), ((), ()))


def dot(a, b, dims=(((1,), (0,)), ((), ()))):
    return lax.dot_general(a, b, dims, preferred_element_type=f32)


def own_shard_mask(s, nq, keys):
    ki = lax.broadcasted_iota(jnp.int32, s.shape, keys)
    qi = lax.broadcasted_iota(jnp.int32, s.shape, 1 - keys)
    return jnp.where((ki >= nq) | (ki <= qi), s, BIG)


def flat(ref, lo, hi):
    return ref[:, 0, :, lo:hi].reshape(ref.shape[0] * ref.shape[2], hi - lo)


def fwd_kernel(causal, groups, q_ref, *refs):
    marks_ref, o_ref, lse_ref = refs[2 * groups :]
    p = pl.program_id(1)
    nq = q_ref.shape[1]
    lane = lax.broadcasted_iota(jnp.int32, (nq, 128), 1)
    q = q_ref[0] * jnp.asarray(0.125, bf16)
    zero = jnp.zeros_like(q)
    outs, lses = [], []
    for h in range(2):
        mine = (lane < 64) if h == 0 else (lane >= 64)
        qc = jnp.concatenate([jnp.where(mine, q, zero), marks_ref[0]], axis=1)
        ss, m = [], None
        for g in range(groups):
            s = dot(qc, jnp.concatenate([flat(refs[2 * g], 0, 128), flat(refs[2 * g + 1], 0, 128)], axis=1), NT)
            if causal and g == 0:
                s = own_shard_mask(s, nq, 1)
            ss.append(s)
            mc = jnp.max(s, axis=1, keepdims=True)
            m = mc if m is None else jnp.maximum(m, mc)
        l, o = 0.0, 0.0
        for g in range(groups):
            e = jnp.exp(ss[g] - m)
            l = l + jnp.sum(e, axis=1, keepdims=True)
            o = o + dot(e.astype(bf16), flat(refs[2 * g], 128, 256))
        outs.append(o / l)
        lses.append(m + jnp.log(l))
    o_ref[0] = jnp.where(lane < 64, outs[0], outs[1])

    @pl.when(p == 0)
    def _():
        lse_ref[...] = jnp.zeros_like(lse_ref)

    lse_ref[0] = jnp.where(lane == 2 * p, lses[0], jnp.where(lane == 2 * p + 1, lses[1], lse_ref[0]))


def call_cost(R, nq, nk, npair, dots):
    return pl.CostEstimate(
        flops=R * npair * 4 * dots * nq * nk * 256,
        bytes_accessed=R * npair * nk * 512,
        transcendentals=R * npair * 2 * nq * nk,
    )


def key_specs(kvs, kmarks):
    specs, args = [], []
    for kv, km in zip(kvs, kmarks):
        S, _, L, _ = kv.shape
        specs.append(pl.BlockSpec((S, 1, L, 256), lambda b, p: (0, b, 0, p)))
        specs.append(pl.BlockSpec((S, 1, L, 128), lambda b, p: (0, b, 0, 0)))
        args += [kv, km]
    return specs, args


def attn_fwd(q, kvs, kmarks, qmarks, causal):
    R, nq, D = q.shape
    npair = D // 128
    each = pl.BlockSpec((1, nq, 128), lambda b, p: (b, 0, p))
    once = pl.BlockSpec((1, nq, 128), lambda b, p: (b, 0, 0))
    specs, args = key_specs(kvs, kmarks)
    nk = sum(kv.shape[0] * kv.shape[2] for kv in kvs)
    return pl.pallas_call(
        functools.partial(fwd_kernel, causal, len(kvs)),
        grid=(R, npair),
        in_specs=[each] + specs + [once],
        out_specs=[each, once],
        out_shape=[jax.ShapeDtypeStruct((R, nq, D), f32), jax.ShapeDtypeStruct((R, nq, 128), f32)],
        compiler_params=pltpu.CompilerParams(vmem_limit_bytes=40 << 20),
        cost_estimate=call_cost(R, nq, nk, npair, 3),
        name="attn_fwd",
    )(q, *args, qmarks)


def split3(x):
    a = x.astype(bf16)
    r = x - a.astype(f32)
    b = r.astype(bf16)
    return a, b, (r - b.astype(f32)).astype(bf16)


def bwd_kernel(causal, groups, q_ref, *refs):
    marks_ref, lse_ref, o_ref, do_ref, dq_ref, dkv_ref = refs[2 * groups :]
    p = pl.program_id(1)
    nq = q_ref.shape[1]
    lane = lax.broadcasted_iota(jnp.int32, (nq, 128), 1)
    q = q_ref[0] * jnp.asarray(0.125, bf16)
    do = do_ref[0]
    zero = jnp.zeros_like(q)
    prod = do.astype(f32) * o_ref[0]
    qc, dc, qm, dm = [], [], [], []
    for h in range(2):
        mine = (lane < 64) if h == 0 else (lane >= 64)
        lse = jnp.sum(jnp.where(lane == 2 * p + h, lse_ref[0], 0.0), axis=1, keepdims=True)
        delta = jnp.sum(jnp.where(mine, prod, 0.0), axis=1, keepdims=True)
        cols, dcols = marks_ref[0], zero
        for k, (a, b) in enumerate(zip(split3(-lse), split3(-delta))):
            cols = jnp.where(lane == 8 + k, a, cols)
            dcols = jnp.where(lane == 8 + k, b, dcols)
        qm.append(jnp.where(mine, q, zero))
        dm.append(jnp.where(mine, do, zero))
        qc.append(jnp.concatenate([qm[h], cols], axis=1))
        dc.append(jnp.concatenate([dm[h], dcols], axis=1))
    qq = jnp.concatenate(qm, axis=0)
    dd = jnp.concatenate(dm, axis=0)
    dq = [0.0, 0.0]
    first = 0
    for g in range(groups):
        S, L = refs[2 * g].shape[0], refs[2 * g].shape[2]
        k, v, km = flat(refs[2 * g], 0, 128), flat(refs[2 * g], 128, 256), flat(refs[2 * g + 1], 0, 128)
        kc = jnp.concatenate([k, km], axis=1)
        vc = jnp.concatenate([v, km], axis=1)
        pts, dss = [], []
        for h in range(2):
            st = dot(kc, qc[h], NT)
            if causal and g == 0:
                st = own_shard_mask(st, nq, 0)
            pt = jnp.exp(st)
            ds = (pt * dot(vc, dc[h], NT)).astype(bf16)
            pts.append(pt.astype(bf16))
            dss.append(ds)
            dq[h] = dq[h] + dot(k, ds, TN)
        dk = dot(jnp.concatenate(dss, axis=1), qq)
        dv = dot(jnp.concatenate(pts, axis=1), dd)
        dkv_ref[first : first + S, 0, :, 0:128] = dk.astype(bf16).reshape(S, L, 128)
        dkv_ref[first : first + S, 0, :, 128:256] = dv.astype(bf16).reshape(S, L, 128)
        first += S
    dq_ref[0] = (jnp.where(lane < 64, dq[0].T, dq[1].T) * 0.125).astype(bf16)


def attn_bwd(q, kvs, kmarks, qmarks, lse, o, do, causal):
    R, nq, D = q.shape
    npair = D // 128
    each = pl.BlockSpec((1, nq, 128), lambda b, p: (b, 0, p))
    once = pl.BlockSpec((1, nq, 128), lambda b, p: (b, 0, 0))
    specs, args = key_specs(kvs, kmarks)
    S, L = sum(kv.shape[0] for kv in kvs), kvs[0].shape[2]
    return pl.pallas_call(
        functools.partial(bwd_kernel, causal, len(kvs)),
        grid=(R, npair),
        in_specs=[each] + specs + [once, once, each, each],
        out_specs=[each, pl.BlockSpec((S, 1, L, 256), lambda b, p: (0, b, 0, p))],
        out_shape=[jax.ShapeDtypeStruct((R, nq, D), bf16), jax.ShapeDtypeStruct((S, R, L, 2 * D), bf16)],
        compiler_params=pltpu.CompilerParams(vmem_limit_bytes=48 << 20),
        cost_estimate=call_cost(R, nq, S * L, npair, 5),
        name="attn_bwd",
    )(q, *args, qmarks, lse, o, do)


def norm_of(r):
    mean = jnp.mean(r, axis=-1, keepdims=True)
    centered = r - mean
    inv = lax.rsqrt(jnp.mean(centered * centered, axis=-1, keepdims=True) + EPS)
    return centered * inv, inv


def norm_grad(dy, unit, inv, gain):
    f = dy * gain
    return (f - jnp.mean(f, axis=-1, keepdims=True) - unit * jnp.mean(f * unit, axis=-1, keepdims=True)) * inv


def total(x):
    return jnp.sum(x.astype(f32), axis=0, keepdims=True)


def ffn_kernel(
    nb, r2_ref, go_ref, up_ref, down_ref, bu_ref, vec_ref,
    out_ref, dr2_ref, do2_ref, gup_ref, gdown_ref, gbu_ref, sums_ref,
    h2_ref, unit_ref, inv_ref, low_ref, act_ref, slope_ref, acc_ref, dz_ref,
):
    t, j = pl.program_id(0), pl.program_id(1)
    g2, s2, bd, g3, s3 = [vec_ref[k : k + 1, :] for k in range(5)]

    @pl.when((t == 0) & (j == 0))
    def _():
        unit, inv = norm_of(r2_ref[...])
        h2 = unit * g2 + s2
        unit_ref[...] = unit
        inv_ref[...] = jnp.broadcast_to(inv, inv_ref.shape)
        low_ref[...] = h2.astype(bf16)
        acc_ref[...] = h2 + bd

    @pl.when(t == 0)
    def _():
        u = dot(low_ref[...], up_ref[...]) + bu_ref[0]
        phi = 0.5 * (1.0 + lax.erf(u * 0.7071067811865476))
        act = (u * phi).astype(bf16)
        act_ref[j] = act
        slope_ref[j] = phi + u * (0.3989422804014327 * jnp.exp(-0.5 * u * u))
        acc_ref[...] += dot(act, down_ref[...])

    @pl.when((t == 0) & (j == nb - 1))
    def _():
        unit, inv = norm_of(acc_ref[...])
        out_ref[...] = (unit * g3 + s3).astype(bf16)
        dy = go_ref[...].astype(f32)
        dr3 = norm_grad(dy, unit, inv, g3)
        dz = dr3.astype(bf16)
        dz_ref[...] = dz
        acc_ref[...] = dr3
        sums_ref[0:1, :] = total(dz)
        sums_ref[1:2, :] = total(dy * unit)
        sums_ref[2:3, :] = total(dy)

    @pl.when(t == 1)
    def _():
        du = (dot(dz_ref[...], down_ref[...], NT) * slope_ref[j]).astype(bf16)
        gbu_ref[0] = total(du)
        gdown_ref[...] = dot(act_ref[j], dz_ref[...], TN).astype(bf16)
        gup_ref[...] = dot(low_ref[...], du, TN).astype(bf16)
        acc_ref[...] += dot(du, up_ref[...], NT)

    @pl.when((t == 1) & (j == nb - 1))
    def _():
        dy = acc_ref[...]
        dr2 = norm_grad(dy, unit_ref[...], inv_ref[:, 0:1], g2)
        do2 = dr2.astype(bf16)
        dr2_ref[...] = dr2
        do2_ref[...] = do2
        sums_ref[3:4, :] = total(dy * unit_ref[...])
        sums_ref[4:5, :] = total(dy)
        sums_ref[5:6, :] = total(do2)


def ffn(r2, go, up, down, bu, vecs):
    T, D = r2.shape
    F = up.shape[1]
    nb = bu.shape[0]
    B = F // nb
    full = lambda a, b: pl.BlockSpec((a, b), lambda t, j: (0, 0))
    shape = jax.ShapeDtypeStruct
    return pl.pallas_call(
        functools.partial(ffn_kernel, nb),
        grid=(2, nb),
        in_specs=[
            full(T, D), full(T, D),
            pl.BlockSpec((D, B), lambda t, j: (0, j)),
            pl.BlockSpec((B, D), lambda t, j: (j, 0)),
            pl.BlockSpec((1, 1, B), lambda t, j: (j, 0, 0)),
            full(8, D),
        ],
        out_specs=[
            full(T, D), full(T, D), full(T, D),
            pl.BlockSpec((D, B), lambda t, j: (0, j * t)),
            pl.BlockSpec((B, D), lambda t, j: (j * t, 0)),
            pl.BlockSpec((1, 1, B), lambda t, j: (j * t, 0, 0)),
            full(8, D),
        ],
        out_shape=[
            shape((T, D), bf16), shape((T, D), f32), shape((T, D), bf16),
            shape((D, F), bf16), shape((F, D), bf16), shape((nb, 1, B), f32), shape((8, D), f32),
        ],
        scratch_shapes=[
            pltpu.VMEM((T, D), f32), pltpu.VMEM((T, D), f32), pltpu.VMEM((T, 128), f32), pltpu.VMEM((T, D), bf16),
            pltpu.VMEM((nb, T, B), bf16), pltpu.VMEM((nb, T, B), f32), pltpu.VMEM((T, D), f32), pltpu.VMEM((T, D), bf16),
        ],
        compiler_params=pltpu.CompilerParams(vmem_limit_bytes=56 << 20),
        cost_estimate=pl.CostEstimate(
            flops=12 * T * D * F, bytes_accessed=32 * T * D + 16 * D * F, transcendentals=2 * T * F
        ),
        name="ffn",
    )(r2, go, up, down, bu, vecs)


def line_place(k, c):
    return k % c, 128 * (k // c)


def lines_of(tile, first, count):
    c, parts = tile.shape[0], []
    while count:
        y, x = line_place(first, c)
        take = min(count, c - y)
        parts.append(tile[y : y + take, x : x + 128])
        first, count = first + take, count - take
    return parts[0] if len(parts) == 1 else jnp.concatenate(parts, axis=0)


def pack_kernel(nvec, *refs):
    mats, vecs, (bu_ref, ids_ref, out_ref, line_ref) = refs[:8], refs[8 : 8 + nvec], refs[8 + nvec :]
    c, D = mats[0].shape
    at = 0
    for group in ((0,), (1, 2), (3,), (4,), (5, 6), (7,)):
        for p in range(D // 128):
            for i in group:
                out_ref[:, at : at + 128] = mats[i][:, p * 128 : (p + 1) * 128].astype(bf16)
                at += 128
    line_ref[...] = jnp.zeros_like(line_ref)
    for k, r in enumerate(vecs + (bu_ref,)):
        y, x = line_place(k, c)
        line_ref[y : y + 1, x : x + r.shape[1]] = r[...]
    for j in range(ids_ref.shape[0]):
        y, x = line_place(nvec + 1 + j, c)
        line_ref[y : y + 1, x : x + 128] = ids_ref[j : j + 1, :].astype(f32)
    out_ref[:, at:] = line_ref[...].astype(bf16)


def pack_weights(mats, vecs, bu, ids):
    c, D = mats[0].shape
    wide = 128 * (-(-(len(vecs) + 1 + ids.shape[0]) // c))
    return pl.pallas_call(
        functools.partial(pack_kernel, len(vecs)),
        out_shape=jax.ShapeDtypeStruct((c, 8 * D + wide), bf16),
        scratch_shapes=[pltpu.VMEM((c, wide), f32)],
        name="pack_weights",
    )(*mats, *[v.reshape(1, c) for v in vecs], bu.reshape(1, -1), ids)


def widen(rows, width, D):
    lane = lax.broadcasted_iota(jnp.int32, rows.shape, 1)
    return jnp.concatenate([jnp.where(lane < width, rows, 0.0), jnp.zeros((rows.shape[0], D - 128), f32)], axis=1)


def spread_kernel(n, nvec, hidden, pairs, line_ref, vec_ref, bu_ref, kv_ref, ids_ref):
    D = vec_ref.shape[1]
    c, w = D // n, hidden * D // n
    vec = jnp.zeros((16, D), f32)
    blocks = [jnp.zeros((8, D), f32) for _ in range(hidden)]
    for d in range(n):
        tile = line_ref[d * c : (d + 1) * c, :].astype(f32)
        rows = jnp.concatenate([lines_of(tile, 0, nvec), jnp.zeros((16 - nvec, 128), f32)], axis=0)
        vec = vec + pltpu.roll(widen(rows, c, D), d * c, axis=1)
        b, at = d * w // D, d * w % D
        row = jnp.concatenate([lines_of(tile, nvec, 1), jnp.zeros((7, 128), f32)], axis=0)
        blocks[b] = blocks[b] + pltpu.roll(widen(row, w, D), at, axis=1)
        ids_ref[d] = lines_of(tile, nvec + 1, ids_ref.shape[1])
    vec_ref[...] = vec
    for k in range(hidden):
        bu_ref[k] = blocks[k][0:1]
    kv_ref[...] = jnp.zeros_like(kv_ref)
    for i, k in enumerate(pairs):
        for p in range(D // 128):
            kv_ref[i : i + 1, p * 256 + 128 : (p + 1) * 256] = vec[k : k + 1, p * 128 : (p + 1) * 128]


def spread_lines(lines, n, nvec, hidden, pairs, nids):
    D = lines.shape[0]
    shape = jax.ShapeDtypeStruct
    return pl.pallas_call(
        functools.partial(spread_kernel, n, nvec, hidden, pairs),
        out_shape=[
            shape((16, D), f32), shape((hidden, 1, D), f32), shape((8, 2 * D), f32), shape((n, nids, 128), f32),
        ],
        name="spread_lines",
    )(lines)


def collect_kernel(n, nvec, hidden, *refs):
    vecs, (bu_ref, out_ref, line_ref) = refs[:nvec], refs[nvec:]
    D = vecs[0].shape[1]
    c, w = D // n, hidden * D // n
    vec = jnp.concatenate([r[...] for r in vecs] + [jnp.zeros((16 - nvec, D), f32)], axis=0)
    line_ref[...] = jnp.zeros_like(line_ref)
    for d in range(n):
        rows = pltpu.roll(vec, (D - d * c) % D, axis=1)[:, 0:128]
        b, at = d * w // D, d * w % D
        row = pltpu.roll(jnp.broadcast_to(bu_ref[b], (8, D)), (D - at) % D, axis=1)[:, 0:128]
        for k in range(nvec + 1):
            y, x = line_place(k, c)
            line_ref[d * c + y : d * c + y + 1, x : x + 128] = rows[k : k + 1] if k < nvec else row[0:1]
    out_ref[...] = line_ref[...].astype(bf16)


def collect_lines(vecs, bu, n):
    D = vecs[0].shape[1]
    c = D // n
    wide = 128 * (-(-(len(vecs) + 1) // c))
    return pl.pallas_call(
        functools.partial(collect_kernel, n, len(vecs), bu.shape[0]),
        out_shape=jax.ShapeDtypeStruct((D, wide), bf16),
        scratch_shapes=[pltpu.VMEM((D, wide), f32)],
        name="collect_lines",
    )(*vecs, bu)


def finish_kernel(nvec, mine_ref, other_ref, *outs):
    mats, vecs, bu_ref = outs[:8], outs[8 : 8 + nvec], outs[8 + nvec]
    c, D = mats[0].shape
    at = 0
    for ref, groups in ((mine_ref, ((0,), (1, 2))), (other_ref, ((4,), (5, 6), (7,), (3,)))):
        at = 0
        for group in groups:
            for p in range(D // 128):
                for i in group:
                    mats[i][:, p * 128 : (p + 1) * 128] = ref[:, at : at + 128].astype(f32)
                    at += 128
    tile = mine_ref[:, 3 * D :].astype(f32)
    for k in range(nvec + 1):
        y, x = line_place(k, c)
        out = vecs[k] if k < nvec else bu_ref
        out[...] = tile[y : y + 1, x : x + out.shape[1]]


def finish(mine, other, D, nvec, width):
    c = mine.shape[0]
    shape = jax.ShapeDtypeStruct
    out = pl.pallas_call(
        functools.partial(finish_kernel, nvec),
        out_shape=[shape((c, D), f32)] * 8 + [shape((1, c), f32)] * nvec + [shape((1, width), f32)],
        name="finish",
    )(mine, other)
    return out[:8], [v.reshape(-1) for v in out[8:]]


BOTH = ("rows", "seq")


def ring_order(n):
    ny = 2 ** ((n.bit_length() - 1) // 2)
    nz = n // ny
    if ny < 2 or nz < 2:
        return list(range(n))
    order = []
    for z in range(nz):
        ys = list(range(1, ny)) if z % 2 == 0 else list(range(ny - 1, 0, -1))
        order += [z * ny + y for y in ys]
    order += [z * ny for z in range(nz - 1, -1, -1)]
    return order


class Ring:
    def __init__(self, n):
        self.n = n
        self.order = ring_order(n)
        self.up = [(self.order[i], self.order[(i + 1) % n]) for i in range(n)]
        self.down = [(b, a) for a, b in self.up]
        self.near = (n - 1) // 2
        self.far = n - 1 - self.near
        self.offsets = [0]
        for d in range(1, self.far + 1):
            self.offsets.append(-d)
            if d <= self.near:
                self.offsets.append(d)
        place = [0] * n
        for i, s in enumerate(self.order):
            place[s] = i
        me = lax.axis_index("seq")
        every = jnp.arange(n, dtype=jnp.int32)
        spot = jnp.sum(jnp.where(every == me, jnp.asarray(place, jnp.int32), 0))
        at = (spot + jnp.asarray(self.offsets, jnp.int32) + n) % n
        self.owners = jnp.sum(jnp.where(at[:, None] == every, jnp.asarray(self.order, jnp.int32), 0), axis=1)

    def arrange(self, x):
        pick = (self.owners[:, None] == jnp.arange(self.n)).reshape((self.n, self.n) + (1,) * (x.ndim - 1))
        return jnp.sum(jnp.where(pick, x[None], 0), axis=1)

    def hop(self, parts):
        low, high = parts[-2] if len(parts) > 1 else parts[-1], parts[-1]
        fresh = [lax.ppermute(low, "seq", self.up)]
        if len(parts) + 1 < self.n:
            fresh.append(lax.ppermute(high, "seq", self.down))
        return parts + fresh

    def open(self, pieces):
        part = dict(zip(self.offsets[-len(pieces) :], pieces))
        return part, part[-self.far], part[self.near] if self.near else None, self.far, self.near

    def step(self, state):
        part, low, high, i, j = state
        if i > 0:
            low = lax.ppermute(low, "seq", self.down)
            i -= 1
            if i:
                low = (low.astype(f32) + part[-i].astype(f32)).astype(bf16)
        if j > i:
            high = lax.ppermute(high, "seq", self.up)
            j -= 1
            if j:
                high = (high.astype(f32) + part[j].astype(f32)).astype(bf16)
        return part, low, high, i, j

    def finish(self, state):
        while state[3] or state[4]:
            state = self.step(state)
        part, low, high, _, _ = state
        total = part[0].astype(f32) + low.astype(f32)
        return total if high is None else total + high.astype(f32)

    def join(self, state, pieces):
        return ({**state[0], **dict(zip(self.offsets, pieces))},) + state[1:]


class Halving:
    def __init__(self, rows, seq):
        self.dims = []
        for axis, n in (("rows", rows), ("seq", seq)):
            for b in range(n.bit_length() - 2, -1, -1):
                self.dims.append((axis, n, b))
        self.order = sorted(range(len(self.dims)), key=lambda i: (self.dims[i][0] != "rows", self.dims[i][2]))

    def open(self, x):
        return x.reshape((2,) * len(self.dims) + (-1, x.shape[-1])), list(range(len(self.dims)))

    def step(self, state):
        x, left = state
        i = next(k for k in self.order if k in left)
        axis, n, b = self.dims[i]
        at = left.index(i)
        mine = (lax.axis_index(axis) >> b) & 1
        keep = lax.dynamic_index_in_dim(x, mine, at, keepdims=False)
        send = lax.dynamic_index_in_dim(x, 1 - mine, at, keepdims=False)
        got = lax.ppermute(send, axis, [(j, j ^ (1 << b)) for j in range(n)])
        return (keep.astype(f32) + got.astype(f32)).astype(bf16), [k for k in left if k != i]

    def finish(self, state):
        while state[1]:
            state = self.step(state)
        return state[0]


def together(*xs):
    return lax.optimization_barrier(xs)


def norm(resid, gain, shift):
    mean = jnp.mean(resid, axis=-1, keepdims=True)
    centered = resid - mean
    inv = lax.rsqrt(jnp.mean(centered * centered, axis=-1, keepdims=True) + EPS)
    unit = centered * inv
    return unit * gain + shift, unit, inv


def norm_back(dy, unit, inv, gain):
    f = dy * gain
    mean = jnp.mean(f, axis=-1, keepdims=True)
    cross = jnp.mean(f * unit, axis=-1, keepdims=True)
    return (f - mean - unit * cross) * inv, jnp.sum(dy * unit, axis=0), jnp.sum(dy, axis=0)


def colsum(x):
    return jnp.sum(x.astype(f32), axis=0)


def key_marks(seg, hidden):
    lane = jnp.arange(128)
    marks = jnp.where(lane < 3, jnp.where(seg[..., None] == lane, 0.0, BIG), 0.0)
    if hidden is not None:
        marks = jnp.where(lane == 3, jnp.where(hidden[..., None], BIG, 0.0), marks)
    return jnp.where((lane >= 8) & (lane <= 10), 1.0, marks).astype(bf16)


def query_marks(seg):
    lane = jnp.arange(128)
    return ((seg[..., None] == lane) | (lane == 3)).astype(bf16)


def row_major(x):
    return with_layout_constraint(x, Layout(tuple(range(x.ndim))))


def layer(nrows, nseq, *args):
    (
        target, memory, target_seg, memory_seg, grad_output,
        self_query, self_qbias, self_key, self_value, self_vbias, self_out, self_obias, norm1_gain, norm1_shift,
        cross_query, cross_qbias, cross_key, cross_value, cross_vbias, cross_out, cross_obias, norm2_gain, norm2_shift,
        ffn_up, ffn_ubias, ffn_down, ffn_dbias, norm3_gain, norm3_shift,
    ) = args
    n = nrows * nseq
    R, L, D = target.shape
    c = self_query.shape[0]
    F = ffn_up.shape[1]
    m = F // D
    ring = Ring(nseq)

    mats = (self_query, self_key, self_value, self_out, cross_query, cross_key, cross_value, cross_out)
    vecs = (
        self_qbias, self_vbias, self_obias, norm1_gain, norm1_shift, cross_qbias, cross_vbias, cross_obias,
        norm2_gain, norm2_shift, ffn_dbias, norm3_gain, norm3_shift,
    )
    nvec = len(vecs)
    ids = jnp.concatenate([target_seg, memory_seg], axis=0).reshape(-1, 128)
    pack = pack_weights(mats, vecs, ffn_ubias, ids)
    everything = lax.all_gather(pack, BOTH, axis=0, tiled=True)
    x = target.reshape(R * L, D)
    parts = [row_major(x)]
    while len(parts) < nseq:
        parts = ring.hop(parts)
    up_rows, down_rows = ffn_up.astype(bf16), ffn_down.astype(bf16)
    everything, up_rows, down_rows, memory, *parts = together(everything, up_rows, down_rows, memory, *parts)
    wanted = ring.hop([row_major(memory.reshape(R * L, D))])
    wup = lax.all_gather(up_rows, BOTH, axis=0, tiled=True)
    wdown = lax.all_gather(down_rows, BOTH, axis=0, tiled=True)
    wq, wkv, wo, cq, ckv, co = [
        everything[:, a * D : b * D] for a, b in ((0, 1), (1, 3), (3, 4), (4, 5), (5, 7), (7, 8))
    ]
    vec, bu, pairs, segs = spread_lines(everything[:, 8 * D :], n, nvec, m, (1, 6), ids.shape[0])
    bq, _, bo, g1, s1, bcq, _, bco, g2, s2, bd, g3, s3 = [vec[k : k + 1] for k in range(nvec)]
    bkv, bckv = pairs[0:1], pairs[1:2]

    segs = segs.reshape(nrows, nseq, 2 * R, L)
    mine = (jnp.arange(nrows) == lax.axis_index("rows")).reshape(nrows, 1, 1, 1)
    segs = ring.arrange(jnp.sum(jnp.where(mine, segs, 0.0), axis=0).astype(jnp.int32))
    hidden = (ring.owners > lax.axis_index("seq"))[:, None, None]
    half = (nseq + 1) // 2
    self_marks = [key_marks(segs[:, :R], hidden)]
    cross_marks = [key_marks(s, None) for s in (segs[:half, R:], segs[half:, R:])]
    marks = query_marks(target_seg)
    halving = Halving(nrows, nseq)

    def rows(t):
        return t.reshape(R, -1, t.shape[-1])

    def pile(parts):
        return row_major(jnp.concatenate(parts, axis=0))

    def project(parts, w, b):
        return (dot(parts, w) + b).astype(bf16).reshape(-1, R, L, 2 * D)

    def pieces(t):
        return list(t.reshape(-1, R, L, D))

    X = pile(parts)
    KV = [project(X, wkv, bkv)]
    Q = rows((dot(x, wq) + bq).astype(bf16))
    Q, KV[0], *wanted = together(Q, KV[0], *wanted)
    wanted = ring.hop(wanted)
    A1, lse1 = attn_fwd(Q, KV, self_marks, marks, True)
    A1, lse1, *wanted = together(A1, lse1, *wanted)
    wanted = ring.hop(wanted)
    a1 = A1.reshape(R * L, D).astype(bf16)
    R1 = x.astype(f32) + dot(a1, wo) + bo
    H1, N1, i1 = norm(R1, g1, s1)
    h1 = H1.astype(bf16)
    CQ = rows((dot(h1, cq) + bcq).astype(bf16))
    while len(wanted) < half:
        wanted = ring.hop(wanted)
    Ms = [pile(wanted[:half])]
    CKV = [project(Ms[0], ckv, bckv)]
    CQ, CKV[0], *wanted = together(CQ, CKV[0], *wanted)
    while len(wanted) < nseq:
        wanted = ring.hop(wanted)
    Ms.append(pile(wanted[half:]))
    CKV.append(project(Ms[1], ckv, bckv))
    A2, lse2 = attn_fwd(CQ, CKV, cross_marks, marks, False)
    a2 = A2.reshape(R * L, D).astype(bf16)
    R2 = H1 + dot(a2, co) + bco

    knobs = jnp.concatenate([vec[8:13], jnp.zeros((3, D), f32)], axis=0)
    output, dR2, dO2, w_up, w_down, dbu, sums = ffn(R2, grad_output.reshape(R * L, D), wup, wdown, bu, knobs)
    output = rows(output)
    gbd, dg3, ds3, dg2, ds2, gbco = [sums[k : k + 1] for k in range(6)]

    up, down = halving.step(halving.open(w_up)), halving.step(halving.open(w_down))
    w_co = dot(a2, dO2, TN).astype(bf16)
    dA2 = dot(dO2, co, NT).astype(bf16)
    dA2, u, d, w_co = together(dA2, up[0], down[0], w_co)
    up, down = halving.step((u, up[1])), halving.step((d, down[1]))
    dCQ, dCKV = attn_bwd(CQ, CKV, cross_marks, marks, lse2, A2, rows(dA2), False)
    dCQ, dCKV = dCQ.reshape(R * L, D), dCKV.reshape(-1, 2 * D)
    dCQ, dCKV, u, d = together(dCQ, dCKV, up[0], down[0])
    up, down = halving.step((u, up[1])), halving.step((d, down[1]))
    dM = dot(dCKV, ckv, NT).astype(bf16)
    dM, dCQ, dCKV = together(dM, dCQ, dCKV)
    to_memory = ring.step(ring.open(pieces(dM)))
    dH1 = dR2 + dot(dCQ, cq, NT)
    dR1, dg1, ds1 = norm_back(dH1, N1, i1, g1)
    dO1 = dR1.astype(bf16)
    dA1 = dot(dO1, wo, NT).astype(bf16)
    near = half * R * L
    w_ckv = (dot(Ms[0], dCKV[:near], TN) + dot(Ms[1], dCKV[near:], TN)).astype(bf16)
    w_cq = dot(h1, dCQ, TN).astype(bf16)
    w_o = dot(a1, dO1, TN).astype(bf16)
    cross_part = jnp.concatenate([w_cq, w_ckv, w_co, w_o], axis=1)
    dA1, cross_part, low, high, u, d = together(dA1, cross_part, to_memory[1], to_memory[2], up[0], down[0])
    up, down = halving.step((u, up[1])), halving.step((d, down[1]))
    to_memory = ring.step(ring.step((to_memory[0], low, high) + to_memory[3:]))
    cross = halving.step(halving.step(halving.open(cross_part)))
    dQ, dKV = attn_bwd(Q, KV, self_marks, marks, lse1, A1, rows(dA1), True)
    dQ, dKV = dQ.reshape(R * L, D), dKV.reshape(-1, 2 * D)
    near = half * R * L
    dX1 = dot(dKV[near:], wkv, NT).astype(bf16)
    dQ, dKV, dX1, low, high, cr, u, d = together(dQ, dKV, dX1, to_memory[1], to_memory[2], cross[0], up[0], down[0])
    to_target = ring.step(ring.open(pieces(dX1)))
    to_memory = (to_memory[0], low, high) + to_memory[3:]
    cross = halving.step((cr, cross[1]))
    dX0 = dot(dKV[:near], wkv, NT).astype(bf16)
    w_kv = dot(X, dKV, TN).astype(bf16)
    w_q = dot(x, dQ, TN).astype(bf16)
    vec_sums = [
        v.reshape(1, D)
        for v in (
            colsum(dQ), colsum(dA1), colsum(dO1), dg1, ds1, colsum(dCQ), colsum(dA2), gbco,
            dg2, ds2, gbd, dg3, ds3,
        )
    ]
    self_part = jnp.concatenate([w_q, w_kv, collect_lines(vec_sums, dbu, n)], axis=1)
    self_part, dX0, low, high, cr = together(self_part, dX0, to_target[1], to_target[2], cross[0])
    to_target = ring.step(ring.join((to_target[0], low, high) + to_target[3:], pieces(dX0)))
    mine = halving.step(halving.open(self_part))
    memory_gradient = ring.finish(to_memory).astype(bf16).reshape(R, L, D)
    cross = (cr, cross[1])
    up, down = (u, up[1]), (d, down[1])
    far = ring.finish(to_target)
    target_gradient = (rows(dR1 + dot(dQ, wq, NT)) + rows(far)).astype(bf16)
    g_up, g_down = halving.finish(up).astype(f32), halving.finish(down).astype(f32)
    grads, small = finish(halving.finish(mine), halving.finish(cross), D, nvec, m * c)
    gq, gk, gv, go, gcq, gck, gcv, gco = grads
    (gbq, gbv, gbo, gg1, gs1, gbcq, gbcv, gbco, gg2, gs2, gbd, gg3, gs3, gbu) = small
    return (
        output, target_gradient, memory_gradient,
        gq, gbq, gk, gv, gbv, go, gbo, gg1, gs1,
        gcq, gbcq, gck, gcv, gbcv, gco, gbco, gg2, gs2,
        g_up, gbu, g_down, gbd, gg3, gs3,
    )


def solution(mesh):
    act, ids, mat, vec = P("rows", "seq", None), P("rows", "seq"), P(BOTH, None), P(BOTH)
    ins = (
        act, act, ids, ids, act,
        mat, vec, mat, mat, vec, mat, vec, vec, vec,
        mat, vec, mat, mat, vec, mat, vec, vec, vec,
        mat, vec, mat, vec, vec, vec,
    )
    outs = (
        act, act, act,
        mat, vec, mat, mat, vec, mat, vec, vec, vec,
        mat, vec, mat, mat, vec, mat, vec, vec, vec,
        mat, vec, mat, vec, vec, vec,
    )
    run = functools.partial(layer, mesh.shape["rows"], mesh.shape["seq"])
    return jax.shard_map(run, mesh=mesh, in_specs=ins, out_specs=outs, check_vma=False)
```

```python
import functools

import jax
import jax.numpy as jnp
from jax import lax
from jax.experimental import pallas as pl
from jax.experimental.pallas import tpu as pltpu
from jax.experimental.layout import Layout, with_layout_constraint
from jax.sharding import PartitionSpec as P

f32 = jnp.float32
bf16 = jnp.bfloat16
EPS = 1e-05
BIG = -1e30
NT = (((1,), (1,)), ((), ()))
TN = (((0,), (0,)), ((), ()))


def dot(a, b, dims=(((1,), (0,)), ((), ()))):
    return lax.dot_general(a, b, dims, preferred_element_type=f32)


def own_shard_mask(s, nq, keys):
    ki = lax.broadcasted_iota(jnp.int32, s.shape, keys)
    qi = lax.broadcasted_iota(jnp.int32, s.shape, 1 - keys)
    return jnp.where((ki >= nq) | (ki <= qi), s, BIG)


def flat(ref, lo, hi):
    return ref[:, 0, :, lo:hi].reshape(ref.shape[0] * ref.shape[2], hi - lo)


def fwd_kernel(causal, groups, q_ref, *refs):
    marks_ref, o_ref, lse_ref = refs[2 * groups :]
    p = pl.program_id(1)
    nq = q_ref.shape[1]
    lane = lax.broadcasted_iota(jnp.int32, (nq, 128), 1)
    q = q_ref[0] * jnp.asarray(0.125, bf16)
    zero = jnp.zeros_like(q)
    outs, lses = [], []
    for h in range(2):
        mine = (lane < 64) if h == 0 else (lane >= 64)
        qc = jnp.concatenate([jnp.where(mine, q, zero), marks_ref[0]], axis=1)
        ss, m = [], None
        for g in range(groups):
            s = dot(qc, jnp.concatenate([flat(refs[2 * g], 0, 128), flat(refs[2 * g + 1], 0, 128)], axis=1), NT)
            if causal and g == 0:
                s = own_shard_mask(s, nq, 1)
            ss.append(s)
            mc = jnp.max(s, axis=1, keepdims=True)
            m = mc if m is None else jnp.maximum(m, mc)
        l, o = 0.0, 0.0
        for g in range(groups):
            e = jnp.exp(ss[g] - m)
            l = l + jnp.sum(e, axis=1, keepdims=True)
            o = o + dot(e.astype(bf16), flat(refs[2 * g], 128, 256))
        outs.append(o / l)
        lses.append(m + jnp.log(l))
    o_ref[0] = jnp.where(lane < 64, outs[0], outs[1])

    @pl.when(p == 0)
    def _():
        lse_ref[...] = jnp.zeros_like(lse_ref)

    lse_ref[0] = jnp.where(lane == 2 * p, lses[0], jnp.where(lane == 2 * p + 1, lses[1], lse_ref[0]))


def call_cost(R, nq, nk, npair, dots):
    return pl.CostEstimate(
        flops=R * npair * 4 * dots * nq * nk * 256,
        bytes_accessed=R * npair * nk * 512,
        transcendentals=R * npair * 2 * nq * nk,
    )


def key_specs(kvs, kmarks):
    specs, args = [], []
    for kv, km in zip(kvs, kmarks):
        S, _, L, _ = kv.shape
        specs.append(pl.BlockSpec((S, 1, L, 256), lambda b, p: (0, b, 0, p)))
        specs.append(pl.BlockSpec((S, 1, L, 128), lambda b, p: (0, b, 0, 0)))
        args += [kv, km]
    return specs, args


def attn_fwd(q, kvs, kmarks, qmarks, causal):
    R, nq, D = q.shape
    npair = D // 128
    each = pl.BlockSpec((1, nq, 128), lambda b, p: (b, 0, p))
    once = pl.BlockSpec((1, nq, 128), lambda b, p: (b, 0, 0))
    specs, args = key_specs(kvs, kmarks)
    nk = sum(kv.shape[0] * kv.shape[2] for kv in kvs)
    return pl.pallas_call(
        functools.partial(fwd_kernel, causal, len(kvs)),
        grid=(R, npair),
        in_specs=[each] + specs + [once],
        out_specs=[each, once],
        out_shape=[jax.ShapeDtypeStruct((R, nq, D), f32), jax.ShapeDtypeStruct((R, nq, 128), f32)],
        compiler_params=pltpu.CompilerParams(vmem_limit_bytes=40 << 20),
        cost_estimate=call_cost(R, nq, nk, npair, 3),
        name="attn_fwd",
    )(q, *args, qmarks)


def split3(x):
    a = x.astype(bf16)
    r = x - a.astype(f32)
    b = r.astype(bf16)
    return a, b, (r - b.astype(f32)).astype(bf16)


def bwd_kernel(causal, groups, first_pair, q_ref, *refs):
    marks_ref, lse_ref, o_ref, do_ref = refs[2 * groups : 2 * groups + 4]
    dq_ref, dkv_ref = refs[-2:]
    p = first_pair + pl.program_id(1)
    nq = q_ref.shape[1]
    lane = lax.broadcasted_iota(jnp.int32, (nq, 128), 1)
    q = q_ref[0] * jnp.asarray(0.125, bf16)
    do = do_ref[0]
    zero = jnp.zeros_like(q)
    prod = do.astype(f32) * o_ref[0]
    qc, dc, qm, dm = [], [], [], []
    for h in range(2):
        mine = (lane < 64) if h == 0 else (lane >= 64)
        lse = jnp.sum(jnp.where(lane == 2 * p + h, lse_ref[0], 0.0), axis=1, keepdims=True)
        delta = jnp.sum(jnp.where(mine, prod, 0.0), axis=1, keepdims=True)
        cols, dcols = marks_ref[0], zero
        for k, (a, b) in enumerate(zip(split3(-lse), split3(-delta))):
            cols = jnp.where(lane == 8 + k, a, cols)
            dcols = jnp.where(lane == 8 + k, b, dcols)
        qm.append(jnp.where(mine, q, zero))
        dm.append(jnp.where(mine, do, zero))
        qc.append(jnp.concatenate([qm[h], cols], axis=1))
        dc.append(jnp.concatenate([dm[h], dcols], axis=1))
    qq = jnp.concatenate(qm, axis=0)
    dd = jnp.concatenate(dm, axis=0)
    dq = [0.0, 0.0]
    first = 0
    for g in range(groups):
        S, L = refs[2 * g].shape[0], refs[2 * g].shape[2]
        k, v, km = flat(refs[2 * g], 0, 128), flat(refs[2 * g], 128, 256), flat(refs[2 * g + 1], 0, 128)
        kc = jnp.concatenate([k, km], axis=1)
        vc = jnp.concatenate([v, km], axis=1)
        pts, dss = [], []
        for h in range(2):
            st = dot(kc, qc[h], NT)
            if causal and g == 0:
                st = own_shard_mask(st, nq, 0)
            pt = jnp.exp(st)
            ds = (pt * dot(vc, dc[h], NT)).astype(bf16)
            pts.append(pt.astype(bf16))
            dss.append(ds)
            dq[h] = dq[h] + dot(k, ds, TN)
        dk = dot(jnp.concatenate(dss, axis=1), qq)
        dv = dot(jnp.concatenate(pts, axis=1), dd)
        dkv_ref[first : first + S, 0, :, 0:128] = dk.astype(bf16).reshape(S, L, 128)
        dkv_ref[first : first + S, 0, :, 128:256] = dv.astype(bf16).reshape(S, L, 128)
        first += S
    dq_ref[0] = (jnp.where(lane < 64, dq[0].T, dq[1].T) * 0.125).astype(bf16)


def attn_bwd(q, kvs, kmarks, qmarks, lse, o, do, causal, first, pairs, into=()):
    R, nq, D = q.shape
    each = pl.BlockSpec((1, nq, 128), lambda b, p: (b, 0, first + p))
    once = pl.BlockSpec((1, nq, 128), lambda b, p: (b, 0, 0))
    specs, args = [], []
    for kv, km in zip(kvs, kmarks):
        S, _, L, _ = kv.shape
        specs.append(pl.BlockSpec((S, 1, L, 256), lambda b, p: (0, b, 0, first + p)))
        specs.append(pl.BlockSpec((S, 1, L, 128), lambda b, p: (0, b, 0, 0)))
        args += [kv, km]
    S, L = sum(kv.shape[0] for kv in kvs), kvs[0].shape[2]
    ins = [q, *args, qmarks, lse, o, do]
    return pl.pallas_call(
        functools.partial(bwd_kernel, causal, len(kvs), first),
        grid=(R, pairs),
        in_specs=[each] + specs + [once, once, each, each] + [pl.BlockSpec(memory_space=pl.ANY) for _ in into],
        out_specs=[each, pl.BlockSpec((S, 1, L, 256), lambda b, p: (0, b, 0, first + p))],
        out_shape=[jax.ShapeDtypeStruct((R, nq, D), bf16), jax.ShapeDtypeStruct((S, R, L, 2 * D), bf16)],
        input_output_aliases={len(ins) + k: k for k in range(len(into))},
        compiler_params=pltpu.CompilerParams(vmem_limit_bytes=48 << 20),
        cost_estimate=call_cost(R, nq, S * L, pairs, 5),
        name="attn_bwd",
    )(*ins, *into)


def norm_of(r):
    mean = jnp.mean(r, axis=-1, keepdims=True)
    centered = r - mean
    inv = lax.rsqrt(jnp.mean(centered * centered, axis=-1, keepdims=True) + EPS)
    return centered * inv, inv


def norm_grad(dy, unit, inv, gain):
    f = dy * gain
    return (f - jnp.mean(f, axis=-1, keepdims=True) - unit * jnp.mean(f * unit, axis=-1, keepdims=True)) * inv


def total(x):
    return jnp.sum(x.astype(f32), axis=0, keepdims=True)


def ffn_kernel(
    nb, r2_ref, go_ref, up_ref, down_ref, bu_ref, vec_ref,
    out_ref, dr2_ref, do2_ref, gup_ref, gdown_ref, gbu_ref, sums_ref,
    h2_ref, unit_ref, inv_ref, low_ref, act_ref, slope_ref, acc_ref, dz_ref,
):
    t, j = pl.program_id(0), pl.program_id(1)
    g2, s2, bd, g3, s3 = [vec_ref[k : k + 1, :] for k in range(5)]

    @pl.when((t == 0) & (j == 0))
    def _():
        unit, inv = norm_of(r2_ref[...])
        h2 = unit * g2 + s2
        unit_ref[...] = unit
        inv_ref[...] = jnp.broadcast_to(inv, inv_ref.shape)
        low_ref[...] = h2.astype(bf16)
        acc_ref[...] = h2 + bd

    @pl.when(t == 0)
    def _():
        u = dot(low_ref[...], up_ref[...]) + bu_ref[0]
        phi = 0.5 * (1.0 + lax.erf(u * 0.7071067811865476))
        act = (u * phi).astype(bf16)
        act_ref[j] = act
        slope_ref[j] = phi + u * (0.3989422804014327 * jnp.exp(-0.5 * u * u))
        acc_ref[...] += dot(act, down_ref[...])

    @pl.when((t == 0) & (j == nb - 1))
    def _():
        unit, inv = norm_of(acc_ref[...])
        out_ref[...] = (unit * g3 + s3).astype(bf16)
        dy = go_ref[...].astype(f32)
        dr3 = norm_grad(dy, unit, inv, g3)
        dz = dr3.astype(bf16)
        dz_ref[...] = dz
        acc_ref[...] = dr3
        sums_ref[0:1, :] = total(dz)
        sums_ref[1:2, :] = total(dy * unit)
        sums_ref[2:3, :] = total(dy)

    @pl.when(t == 1)
    def _():
        du = (dot(dz_ref[...], down_ref[...], NT) * slope_ref[j]).astype(bf16)
        gbu_ref[0] = total(du)
        gdown_ref[...] = dot(act_ref[j], dz_ref[...], TN).astype(bf16)
        gup_ref[...] = dot(low_ref[...], du, TN).astype(bf16)
        acc_ref[...] += dot(du, up_ref[...], NT)

    @pl.when((t == 1) & (j == nb - 1))
    def _():
        dy = acc_ref[...]
        dr2 = norm_grad(dy, unit_ref[...], inv_ref[:, 0:1], g2)
        do2 = dr2.astype(bf16)
        dr2_ref[...] = dr2
        do2_ref[...] = do2
        sums_ref[3:4, :] = total(dy * unit_ref[...])
        sums_ref[4:5, :] = total(dy)
        sums_ref[5:6, :] = total(do2)


def ffn(r2, go, up, down, bu, vecs):
    T, D = r2.shape
    F = up.shape[1]
    nb = bu.shape[0]
    B = F // nb
    full = lambda a, b: pl.BlockSpec((a, b), lambda t, j: (0, 0))
    shape = jax.ShapeDtypeStruct
    return pl.pallas_call(
        functools.partial(ffn_kernel, nb),
        grid=(2, nb),
        in_specs=[
            full(T, D), full(T, D),
            pl.BlockSpec((D, B), lambda t, j: (0, j)),
            pl.BlockSpec((B, D), lambda t, j: (j, 0)),
            pl.BlockSpec((1, 1, B), lambda t, j: (j, 0, 0)),
            full(8, D),
        ],
        out_specs=[
            full(T, D), full(T, D), full(T, D),
            pl.BlockSpec((D, B), lambda t, j: (0, j * t)),
            pl.BlockSpec((B, D), lambda t, j: (j * t, 0)),
            pl.BlockSpec((1, 1, B), lambda t, j: (j * t, 0, 0)),
            full(8, D),
        ],
        out_shape=[
            shape((T, D), bf16), shape((T, D), f32), shape((T, D), bf16),
            shape((D, F), bf16), shape((F, D), bf16), shape((nb, 1, B), f32), shape((8, D), f32),
        ],
        scratch_shapes=[
            pltpu.VMEM((T, D), f32), pltpu.VMEM((T, D), f32), pltpu.VMEM((T, 128), f32), pltpu.VMEM((T, D), bf16),
            pltpu.VMEM((nb, T, B), bf16), pltpu.VMEM((nb, T, B), f32), pltpu.VMEM((T, D), f32), pltpu.VMEM((T, D), bf16),
        ],
        compiler_params=pltpu.CompilerParams(vmem_limit_bytes=56 << 20),
        cost_estimate=pl.CostEstimate(
            flops=12 * T * D * F, bytes_accessed=32 * T * D + 16 * D * F, transcendentals=2 * T * F
        ),
        name="ffn",
    )(r2, go, up, down, bu, vecs)


def line_place(k, c):
    return k % c, 128 * (k // c)


def lines_of(tile, first, count):
    c, parts = tile.shape[0], []
    while count:
        y, x = line_place(first, c)
        take = min(count, c - y)
        parts.append(tile[y : y + take, x : x + 128])
        first, count = first + take, count - take
    return parts[0] if len(parts) == 1 else jnp.concatenate(parts, axis=0)


def pack_kernel(nvec, *refs):
    mats, vecs, (bu_ref, ids_ref, out_ref, line_ref) = refs[:8], refs[8 : 8 + nvec], refs[8 + nvec :]
    c, D = mats[0].shape
    at = 0
    for group in ((0,), (1, 2), (3,), (4,), (5, 6), (7,)):
        for p in range(D // 128):
            for i in group:
                out_ref[:, at : at + 128] = mats[i][:, p * 128 : (p + 1) * 128].astype(bf16)
                at += 128
    line_ref[...] = jnp.zeros_like(line_ref)
    for k, r in enumerate(vecs + (bu_ref,)):
        y, x = line_place(k, c)
        line_ref[y : y + 1, x : x + r.shape[1]] = r[...]
    for j in range(ids_ref.shape[0]):
        y, x = line_place(nvec + 1 + j, c)
        line_ref[y : y + 1, x : x + 128] = ids_ref[j : j + 1, :].astype(f32)
    out_ref[:, at:] = line_ref[...].astype(bf16)


def pack_weights(mats, vecs, bu, ids):
    c, D = mats[0].shape
    wide = 128 * (-(-(len(vecs) + 1 + ids.shape[0]) // c))
    return pl.pallas_call(
        functools.partial(pack_kernel, len(vecs)),
        out_shape=jax.ShapeDtypeStruct((c, 8 * D + wide), bf16),
        scratch_shapes=[pltpu.VMEM((c, wide), f32)],
        name="pack_weights",
    )(*mats, *[v.reshape(1, c) for v in vecs], bu.reshape(1, -1), ids)


def widen(rows, width, D):
    lane = lax.broadcasted_iota(jnp.int32, rows.shape, 1)
    return jnp.concatenate([jnp.where(lane < width, rows, 0.0), jnp.zeros((rows.shape[0], D - 128), f32)], axis=1)


def spread_kernel(n, nvec, hidden, pairs, line_ref, vec_ref, bu_ref, kv_ref, ids_ref):
    D = vec_ref.shape[1]
    c, w = D // n, hidden * D // n
    vec = jnp.zeros((16, D), f32)
    blocks = [jnp.zeros((8, D), f32) for _ in range(hidden)]
    for d in range(n):
        tile = line_ref[d * c : (d + 1) * c, :].astype(f32)
        rows = jnp.concatenate([lines_of(tile, 0, nvec), jnp.zeros((16 - nvec, 128), f32)], axis=0)
        vec = vec + pltpu.roll(widen(rows, c, D), d * c, axis=1)
        b, at = d * w // D, d * w % D
        row = jnp.concatenate([lines_of(tile, nvec, 1), jnp.zeros((7, 128), f32)], axis=0)
        blocks[b] = blocks[b] + pltpu.roll(widen(row, w, D), at, axis=1)
        ids_ref[d] = lines_of(tile, nvec + 1, ids_ref.shape[1])
    vec_ref[...] = vec
    for k in range(hidden):
        bu_ref[k] = blocks[k][0:1]
    kv_ref[...] = jnp.zeros_like(kv_ref)
    for i, k in enumerate(pairs):
        for p in range(D // 128):
            kv_ref[i : i + 1, p * 256 + 128 : (p + 1) * 256] = vec[k : k + 1, p * 128 : (p + 1) * 128]


def spread_lines(lines, n, nvec, hidden, pairs, nids):
    D = lines.shape[0]
    shape = jax.ShapeDtypeStruct
    return pl.pallas_call(
        functools.partial(spread_kernel, n, nvec, hidden, pairs),
        out_shape=[
            shape((16, D), f32), shape((hidden, 1, D), f32), shape((8, 2 * D), f32), shape((n, nids, 128), f32),
        ],
        name="spread_lines",
    )(lines)


def collect_kernel(n, nvec, hidden, *refs):
    vecs, (bu_ref, out_ref, line_ref) = refs[:nvec], refs[nvec:]
    D = vecs[0].shape[1]
    c, w = D // n, hidden * D // n
    vec = jnp.concatenate([r[...] for r in vecs] + [jnp.zeros((16 - nvec, D), f32)], axis=0)
    line_ref[...] = jnp.zeros_like(line_ref)
    for d in range(n):
        rows = pltpu.roll(vec, (D - d * c) % D, axis=1)[:, 0:128]
        b, at = d * w // D, d * w % D
        row = pltpu.roll(jnp.broadcast_to(bu_ref[b], (8, D)), (D - at) % D, axis=1)[:, 0:128]
        for k in range(nvec + 1):
            y, x = line_place(k, c)
            line_ref[d * c + y : d * c + y + 1, x : x + 128] = rows[k : k + 1] if k < nvec else row[0:1]
    out_ref[...] = line_ref[...].astype(bf16)


def collect_lines(vecs, bu, n):
    D = vecs[0].shape[1]
    c = D // n
    wide = 128 * (-(-(len(vecs) + 1) // c))
    return pl.pallas_call(
        functools.partial(collect_kernel, n, len(vecs), bu.shape[0]),
        out_shape=jax.ShapeDtypeStruct((D, wide), bf16),
        scratch_shapes=[pltpu.VMEM((D, wide), f32)],
        name="collect_lines",
    )(*vecs, bu)


def finish_kernel(nvec, cut, mine_ref, other_ref, *outs):
    mats, vecs, bu_ref = outs[:8], outs[8 : 8 + nvec], outs[8 + nvec]
    c, D = mats[0].shape
    full = D // 128
    for ref, groups in (
        (mine_ref, (((0,), 0, full), ((1, 2), cut, full))),
        (other_ref, (((4,), 0, full), ((5, 6), 0, full), ((7,), 0, full), ((3,), 0, full), ((1, 2), 0, cut))),
    ):
        at = 0
        for group, start, stop in groups:
            for p in range(start, stop):
                for i in group:
                    mats[i][:, p * 128 : (p + 1) * 128] = ref[:, at : at + 128].astype(f32)
                    at += 128
    tile = mine_ref[:, D + 256 * (full - cut) :].astype(f32)
    for k in range(nvec + 1):
        y, x = line_place(k, c)
        out = vecs[k] if k < nvec else bu_ref
        out[...] = tile[y : y + 1, x : x + out.shape[1]]


def finish(mine, other, D, nvec, width, cut):
    c = mine.shape[0]
    shape = jax.ShapeDtypeStruct
    out = pl.pallas_call(
        functools.partial(finish_kernel, nvec, cut),
        out_shape=[shape((c, D), f32)] * 8 + [shape((1, c), f32)] * nvec + [shape((1, width), f32)],
        name="finish",
    )(mine, other)
    return out[:8], [v.reshape(-1) for v in out[8:]]


BOTH = ("rows", "seq")


def ring_order(n):
    ny = 2 ** ((n.bit_length() - 1) // 2)
    nz = n // ny
    if ny < 2 or nz < 2:
        return list(range(n))
    order = []
    for z in range(nz):
        ys = list(range(1, ny)) if z % 2 == 0 else list(range(ny - 1, 0, -1))
        order += [z * ny + y for y in ys]
    order += [z * ny for z in range(nz - 1, -1, -1)]
    return order


class Ring:
    def __init__(self, n):
        self.n = n
        self.order = ring_order(n)
        self.up = [(self.order[i], self.order[(i + 1) % n]) for i in range(n)]
        self.down = [(b, a) for a, b in self.up]
        self.near = (n - 1) // 2
        self.far = n - 1 - self.near
        self.offsets = [0]
        for d in range(1, self.far + 1):
            self.offsets.append(-d)
            if d <= self.near:
                self.offsets.append(d)
        place = [0] * n
        for i, s in enumerate(self.order):
            place[s] = i
        me = lax.axis_index("seq")
        every = jnp.arange(n, dtype=jnp.int32)
        spot = jnp.sum(jnp.where(every == me, jnp.asarray(place, jnp.int32), 0))
        at = (spot + jnp.asarray(self.offsets, jnp.int32) + n) % n
        self.owners = jnp.sum(jnp.where(at[:, None] == every, jnp.asarray(self.order, jnp.int32), 0), axis=1)

    def arrange(self, x):
        pick = (self.owners[:, None] == jnp.arange(self.n)).reshape((self.n, self.n) + (1,) * (x.ndim - 1))
        return jnp.sum(jnp.where(pick, x[None], 0), axis=1)

    def hop(self, parts):
        low, high = parts[-2] if len(parts) > 1 else parts[-1], parts[-1]
        fresh = [lax.ppermute(low, "seq", self.up)]
        if len(parts) + 1 < self.n:
            fresh.append(lax.ppermute(high, "seq", self.down))
        return parts + fresh


class RingSum:
    def __init__(self, ring, last):
        self.ring, self.i, self.j = ring, ring.far, ring.near
        self.part = dict(zip(ring.offsets[-len(last) :], last))
        self.held = [self.part[-self.i], self.part[self.j]]

    def join(self, terms):
        self.part.update(zip(self.ring.offsets, terms))

    def add(self, moved, at, left):
        return (moved.astype(f32) + self.part[at].astype(f32)).astype(bf16) if left else moved

    def step(self):
        if self.j >= self.i > 0:
            self.j -= 1
            self.held[1] = self.add(lax.ppermute(self.held[1], "seq", self.ring.up), self.j, self.j)
        if self.i > 0:
            self.i -= 1
            self.held[0] = self.add(lax.ppermute(self.held[0], "seq", self.ring.down), -self.i, self.i)

    def finish(self):
        while self.i or self.j:
            self.step()
        return sum((h.astype(f32) for h in self.held), self.part[0].astype(f32))


class Halving:
    def __init__(self, rows, seq, x, early=None):
        self.rows, self.bits = rows, rows.bit_length() - 1
        self.steps = list(range(self.bits))
        self.steps.insert(self.bits if early is None else min(early, self.bits), "seq")
        self.left, self.open = self.bits, False
        self.held = [x.reshape((2,) * self.bits + (seq, -1, x.shape[-1]))]

    def settle(self, kind):
        x = self.held[0]
        if self.open:
            self.open = False
            return jnp.sum(x.astype(f32), axis=self.left).astype(kind)
        return x.astype(kind)

    def step(self):
        x, b = self.settle(bf16), self.steps.pop(0)
        if b == "seq":
            self.held, self.open = [lax.all_to_all(x, "seq", self.left, self.left)], True
            return
        self.left -= 1
        mine = (lax.axis_index("rows") >> b) & 1
        keep = lax.dynamic_index_in_dim(x, mine, self.left, keepdims=False)
        send = lax.dynamic_index_in_dim(x, 1 - mine, self.left, keepdims=False)
        got = lax.ppermute(send, "rows", [(j, j ^ (1 << b)) for j in range(self.rows)])
        self.held = [(keep.astype(f32) + got.astype(f32)).astype(bf16)]

    def finish(self):
        while self.steps:
            self.step()
        return self.settle(f32)


def slot(values, *moving):
    held = [h for m in moving for h in m.held]
    out = list(lax.optimization_barrier(tuple(values) + tuple(held)))
    for m in reversed(moving):
        m.held = out[-len(m.held) :]
        del out[-len(m.held) :]
    return out


def together(*xs):
    return lax.optimization_barrier(xs)


def norm(resid, gain, shift):
    mean = jnp.mean(resid, axis=-1, keepdims=True)
    centered = resid - mean
    inv = lax.rsqrt(jnp.mean(centered * centered, axis=-1, keepdims=True) + EPS)
    unit = centered * inv
    return unit * gain + shift, unit, inv


def norm_back(dy, unit, inv, gain):
    f = dy * gain
    mean = jnp.mean(f, axis=-1, keepdims=True)
    cross = jnp.mean(f * unit, axis=-1, keepdims=True)
    return (f - mean - unit * cross) * inv, jnp.sum(dy * unit, axis=0), jnp.sum(dy, axis=0)


def colsum(x):
    return jnp.sum(x.astype(f32), axis=0)


def key_marks(seg, hidden):
    lane = jnp.arange(128)
    marks = jnp.where(lane < 3, jnp.where(seg[..., None] == lane, 0.0, BIG), 0.0)
    if hidden is not None:
        marks = jnp.where(lane == 3, jnp.where(hidden[..., None], BIG, 0.0), marks)
    return jnp.where((lane >= 8) & (lane <= 10), 1.0, marks).astype(bf16)


def query_marks(seg):
    lane = jnp.arange(128)
    return ((seg[..., None] == lane) | (lane == 3)).astype(bf16)


def row_major(x):
    return with_layout_constraint(x, Layout(tuple(range(x.ndim))))


def layer(nrows, nseq, *args):
    (
        target, memory, target_seg, memory_seg, grad_output,
        self_query, self_qbias, self_key, self_value, self_vbias, self_out, self_obias, norm1_gain, norm1_shift,
        cross_query, cross_qbias, cross_key, cross_value, cross_vbias, cross_out, cross_obias, norm2_gain, norm2_shift,
        ffn_up, ffn_ubias, ffn_down, ffn_dbias, norm3_gain, norm3_shift,
    ) = args
    n = nrows * nseq
    R, L, D = target.shape
    c = self_query.shape[0]
    F = ffn_up.shape[1]
    m = F // D
    ring = Ring(nseq)

    mats = (self_query, self_key, self_value, self_out, cross_query, cross_key, cross_value, cross_out)
    vecs = (
        self_qbias, self_vbias, self_obias, norm1_gain, norm1_shift, cross_qbias, cross_vbias, cross_obias,
        norm2_gain, norm2_shift, ffn_dbias, norm3_gain, norm3_shift,
    )
    nvec = len(vecs)
    ids = jnp.concatenate([target_seg, memory_seg], axis=0).reshape(-1, 128)
    pack = pack_weights(mats, vecs, ffn_ubias, ids)
    everything = lax.all_gather(pack, BOTH, axis=0, tiled=True)
    x = target.reshape(R * L, D)
    parts = [row_major(x)]
    while len(parts) < nseq:
        parts = ring.hop(parts)
    up_rows, down_rows = ffn_up.astype(bf16), ffn_down.astype(bf16)
    everything, up_rows, down_rows, memory, *parts = together(everything, up_rows, down_rows, memory, *parts)
    wanted = ring.hop([row_major(memory.reshape(R * L, D))])
    wup = lax.all_gather(up_rows, BOTH, axis=0, tiled=True)
    wdown = lax.all_gather(down_rows, BOTH, axis=0, tiled=True)
    wq, wkv, wo, cq, ckv, co = [
        everything[:, a * D : b * D] for a, b in ((0, 1), (1, 3), (3, 4), (4, 5), (5, 7), (7, 8))
    ]
    vec, bu, pairs, segs = spread_lines(everything[:, 8 * D :], n, nvec, m, (1, 6), ids.shape[0])
    bq, _, bo, g1, s1, bcq, _, bco, g2, s2, bd, g3, s3 = [vec[k : k + 1] for k in range(nvec)]
    bkv, bckv = pairs[0:1], pairs[1:2]

    segs = segs.reshape(nrows, nseq, 2 * R, L)
    mine = (jnp.arange(nrows) == lax.axis_index("rows")).reshape(nrows, 1, 1, 1)
    segs = ring.arrange(jnp.sum(jnp.where(mine, segs, 0.0), axis=0).astype(jnp.int32))
    hidden = (ring.owners > lax.axis_index("seq"))[:, None, None]
    half = (nseq + 1) // 2
    self_marks = [key_marks(segs[:, :R], hidden)]
    cross_marks = [key_marks(s, None) for s in (segs[:half, R:], segs[half:, R:])]
    marks = query_marks(target_seg)

    def rows(t):
        return t.reshape(R, -1, t.shape[-1])

    def pile(parts):
        return row_major(jnp.concatenate(parts, axis=0))

    def project(parts, w, b):
        return (dot(parts, w) + b).astype(bf16).reshape(-1, R, L, 2 * D)

    def pieces(t):
        return list(t.reshape(-1, R, L, D))

    X = pile(parts)
    KV = [project(X, wkv, bkv)]
    Q = rows((dot(x, wq) + bq).astype(bf16))
    Q, KV[0], *wanted = together(Q, KV[0], *wanted)
    wanted = ring.hop(wanted)
    A1, lse1 = attn_fwd(Q, KV, self_marks, marks, True)
    A1, lse1, *wanted = together(A1, lse1, *wanted)
    wanted = ring.hop(wanted)
    a1 = A1.reshape(R * L, D).astype(bf16)
    R1 = x.astype(f32) + dot(a1, wo) + bo
    H1, N1, i1 = norm(R1, g1, s1)
    h1 = H1.astype(bf16)
    CQ = rows((dot(h1, cq) + bcq).astype(bf16))
    while len(wanted) < half:
        wanted = ring.hop(wanted)
    Ms = [pile(wanted[:half])]
    CKV = [project(Ms[0], ckv, bckv)]
    CQ, CKV[0], *wanted = together(CQ, CKV[0], *wanted)
    while len(wanted) < nseq:
        wanted = ring.hop(wanted)
    Ms.append(pile(wanted[half:]))
    CKV.append(project(Ms[1], ckv, bckv))
    A2, lse2 = attn_fwd(CQ, CKV, cross_marks, marks, False)
    a2 = A2.reshape(R * L, D).astype(bf16)
    R2 = H1 + dot(a2, co) + bco

    knobs = jnp.concatenate([vec[8:13], jnp.zeros((3, D), f32)], axis=0)
    output, dR2, dO2, w_up, w_down, dbu, sums = ffn(R2, grad_output.reshape(R * L, D), wup, wdown, bu, knobs)
    output = rows(output)
    gbd, dg3, ds3, dg2, ds2, gbco = [sums[k : k + 1] for k in range(6)]

    def halved(w, early=None):
        return Halving(nrows, nseq, w, early)

    def scattered(w):
        return lax.psum_scatter(w, BOTH, scatter_dimension=0, tiled=True)

    npair = D // 128
    cuts = (0, npair // 3, 2 * npair // 3, npair)
    near = half * R * L
    shares = [w_up[:, k * D : (k + 1) * D].reshape(n, c, D) for k in range(m)] + [w_down.reshape(n, m * c, D)]
    dO2, ffn_part = slot([dO2, jnp.concatenate(shares, axis=1).reshape(-1, D)])
    g_ffn = scattered(ffn_part)
    w_co = dot(a2, dO2, TN).astype(bf16)
    dA2 = rows(dot(dO2, co, NT).astype(bf16))
    dA2, w_co = slot([dA2, w_co])
    dCQ, dCKV = slot(attn_bwd(CQ, CKV, cross_marks, marks, lse2, A2, dA2, False, 0, npair))
    g = dCKV.reshape(-1, 2 * D)
    dM = dot(g, ckv, NT).astype(bf16)
    dCQ = dCQ.reshape(R * L, D)
    dM, dCQ, g = slot([dM, dCQ, g])
    to_memory = RingSum(ring, pieces(dM))
    to_memory.step()
    w_ckv = (dot(Ms[0], g[:near], TN) + dot(Ms[1], g[near:], TN)).astype(bf16)
    dCQ, w_ckv = slot([dCQ, w_ckv])
    w_cq = dot(h1, dCQ, TN).astype(bf16)
    dH1 = dR2 + dot(dCQ, cq, NT)
    dR1, dg1, ds1 = norm_back(dH1, N1, i1, g1)
    dO1 = dR1.astype(bf16)
    dA1 = rows(dot(dO1, wo, NT).astype(bf16))
    w_o = dot(a1, dO1, TN).astype(bf16)
    dA1, w_o, w_cq = slot([dA1, w_o, w_cq], to_memory)
    own = (Q, KV, self_marks, marks, lse1, A1, dA1, True)
    sent, w_kv, into = [w_cq, w_ckv, w_co, w_o], [], ()
    for k in range(3):
        to_memory.step()
        at, count = cuts[k], cuts[k + 1] - cuts[k]
        into = slot(attn_bwd(*own, at, count, into), *([to_memory] if k == 2 else []))
        if k < 2:
            w_kv.append(dot(X, into[1].reshape(-1, 2 * D)[:, 256 * at : 256 * (at + count)], TN).astype(bf16))
            if k == 1:
                into = slot([*into, jnp.concatenate(sent + w_kv, axis=1), g_ffn], to_memory)
                others, g_ffn = scattered(into[2]), into[3]
                into = into[:2]
            else:
                *into, w_kv[0] = slot([*into, w_kv[0]], to_memory)
    to_memory.step()
    dQ, dKV = into
    g = dKV.reshape(-1, 2 * D)
    dQ = dQ.reshape(R * L, D)
    dX = dot(g, wkv, NT).astype(bf16)
    g, dQ, dX = slot([g, dQ, dX])
    to_target = RingSum(ring, pieces(dX))
    to_target.step()
    w_kv2 = dot(X, g[:, 256 * cuts[2] :], TN).astype(bf16)
    w_q = dot(x, dQ, TN).astype(bf16)
    vec_sums = [
        v.reshape(1, D)
        for v in (
            colsum(dQ), colsum(dA1.reshape(R * L, D)), colsum(dO1), dg1, ds1,
            colsum(dCQ), colsum(dA2.reshape(R * L, D)), gbco, dg2, ds2, gbd, dg3, ds3,
        )
    ]
    late = jnp.concatenate([w_q, w_kv2, collect_lines(vec_sums, dbu, n)], axis=1)
    (late,) = slot([late], to_target)
    late = halved(late)
    late.step()
    to_target.step()
    late.step()
    to_target.step()
    late.step()
    target_gradient = (rows(dR1 + dot(dQ, wq, NT)) + rows(to_target.finish())).astype(bf16)
    memory_gradient = to_memory.finish().astype(bf16).reshape(R, L, D)
    g_up = jnp.concatenate([g_ffn[k * c : (k + 1) * c] for k in range(m)], axis=1).astype(f32)
    g_down = g_ffn[m * c :].astype(f32)
    grads, small = finish(late.finish(), others, D, nvec, m * c, cuts[2])
    gq, gk, gv, go, gcq, gck, gcv, gco = grads
    (gbq, gbv, gbo, gg1, gs1, gbcq, gbcv, gbco, gg2, gs2, gbd, gg3, gs3, gbu) = small
    return (
        output, target_gradient, memory_gradient,
        gq, gbq, gk, gv, gbv, go, gbo, gg1, gs1,
        gcq, gbcq, gck, gcv, gbcv, gco, gbco, gg2, gs2,
        g_up, gbu, g_down, gbd, gg3, gs3,
    )


def solution(mesh):
    act, ids, mat, vec = P("rows", "seq", None), P("rows", "seq"), P(BOTH, None), P(BOTH)
    ins = (
        act, act, ids, ids, act,
        mat, vec, mat, mat, vec, mat, vec, vec, vec,
        mat, vec, mat, mat, vec, mat, vec, vec, vec,
        mat, vec, mat, vec, vec, vec,
    )
    outs = (
        act, act, act,
        mat, vec, mat, mat, vec, mat, vec, vec, vec,
        mat, vec, mat, mat, vec, mat, vec, vec, vec,
        mat, vec, mat, vec, vec, vec,
    )
    run = functools.partial(layer, mesh.shape["rows"], mesh.shape["seq"])
    return jax.shard_map(run, mesh=mesh, in_specs=ins, out_specs=outs, check_vma=False)
```

```python
import functools

import jax
import jax.numpy as jnp
from jax import lax
from jax.experimental import pallas as pl
from jax.experimental.pallas import tpu as pltpu
from jax.experimental.layout import Layout, with_layout_constraint
from jax.sharding import PartitionSpec as P

f32 = jnp.float32
bf16 = jnp.bfloat16
EPS = 1e-05
BIG = -1e30
NT = (((1,), (1,)), ((), ()))
TN = (((0,), (0,)), ((), ()))


def dot(a, b, dims=(((1,), (0,)), ((), ()))):
    return lax.dot_general(a, b, dims, preferred_element_type=f32)


def own_shard_mask(s, nq, keys):
    ki = lax.broadcasted_iota(jnp.int32, s.shape, keys)
    qi = lax.broadcasted_iota(jnp.int32, s.shape, 1 - keys)
    return jnp.where((ki >= nq) | (ki <= qi), s, BIG)


def flat(ref, lo, hi):
    return ref[:, 0, :, lo:hi].reshape(ref.shape[0] * ref.shape[2], hi - lo)


def fwd_kernel(causal, groups, q_ref, *refs):
    marks_ref, o_ref, lse_ref = refs[2 * groups :]
    p = pl.program_id(1)
    nq = q_ref.shape[1]
    lane = lax.broadcasted_iota(jnp.int32, (nq, 128), 1)
    q = q_ref[0] * jnp.asarray(0.125, bf16)
    zero = jnp.zeros_like(q)
    outs, lses = [], []
    for h in range(2):
        mine = (lane < 64) if h == 0 else (lane >= 64)
        qc = jnp.concatenate([jnp.where(mine, q, zero), marks_ref[0]], axis=1)
        ss, m = [], None
        for g in range(groups):
            s = dot(qc, jnp.concatenate([flat(refs[2 * g], 0, 128), flat(refs[2 * g + 1], 0, 128)], axis=1), NT)
            if causal and g == 0:
                s = own_shard_mask(s, nq, 1)
            ss.append(s)
            mc = jnp.max(s, axis=1, keepdims=True)
            m = mc if m is None else jnp.maximum(m, mc)
        l, o = 0.0, 0.0
        for g in range(groups):
            e = jnp.exp(ss[g] - m)
            l = l + jnp.sum(e, axis=1, keepdims=True)
            o = o + dot(e.astype(bf16), flat(refs[2 * g], 128, 256))
        outs.append(o / l)
        lses.append(m + jnp.log(l))
    o_ref[0] = jnp.where(lane < 64, outs[0], outs[1])

    @pl.when(p == 0)
    def _():
        lse_ref[...] = jnp.zeros_like(lse_ref)

    lse_ref[0] = jnp.where(lane == 2 * p, lses[0], jnp.where(lane == 2 * p + 1, lses[1], lse_ref[0]))


def call_cost(R, nq, nk, npair, dots):
    return pl.CostEstimate(
        flops=R * npair * 4 * dots * nq * nk * 256,
        bytes_accessed=R * npair * nk * 512,
        transcendentals=R * npair * 2 * nq * nk,
    )


def key_specs(kvs, kmarks):
    specs, args = [], []
    for kv, km in zip(kvs, kmarks):
        S, _, L, _ = kv.shape
        specs.append(pl.BlockSpec((S, 1, L, 256), lambda b, p: (0, b, 0, p)))
        specs.append(pl.BlockSpec((S, 1, L, 128), lambda b, p: (0, b, 0, 0)))
        args += [kv, km]
    return specs, args


def attn_fwd(q, kvs, kmarks, qmarks, causal):
    R, nq, D = q.shape
    npair = D // 128
    each = pl.BlockSpec((1, nq, 128), lambda b, p: (b, 0, p))
    once = pl.BlockSpec((1, nq, 128), lambda b, p: (b, 0, 0))
    specs, args = key_specs(kvs, kmarks)
    nk = sum(kv.shape[0] * kv.shape[2] for kv in kvs)
    return pl.pallas_call(
        functools.partial(fwd_kernel, causal, len(kvs)),
        grid=(R, npair),
        in_specs=[each] + specs + [once],
        out_specs=[each, once],
        out_shape=[jax.ShapeDtypeStruct((R, nq, D), f32), jax.ShapeDtypeStruct((R, nq, 128), f32)],
        compiler_params=pltpu.CompilerParams(vmem_limit_bytes=40 << 20),
        cost_estimate=call_cost(R, nq, nk, npair, 3),
        name="attn_fwd",
    )(q, *args, qmarks)


def split3(x):
    a = x.astype(bf16)
    r = x - a.astype(f32)
    b = r.astype(bf16)
    return a, b, (r - b.astype(f32)).astype(bf16)


def bwd_kernel(causal, groups, first_pair, q_ref, *refs):
    marks_ref, lse_ref, o_ref, do_ref = refs[2 * groups : 2 * groups + 4]
    dq_ref, dkv_ref = refs[-2:]
    p = first_pair + pl.program_id(1)
    nq = q_ref.shape[1]
    lane = lax.broadcasted_iota(jnp.int32, (nq, 128), 1)
    q = q_ref[0] * jnp.asarray(0.125, bf16)
    do = do_ref[0]
    zero = jnp.zeros_like(q)
    prod = do.astype(f32) * o_ref[0]
    qc, dc, qm, dm = [], [], [], []
    for h in range(2):
        mine = (lane < 64) if h == 0 else (lane >= 64)
        lse = jnp.sum(jnp.where(lane == 2 * p + h, lse_ref[0], 0.0), axis=1, keepdims=True)
        delta = jnp.sum(jnp.where(mine, prod, 0.0), axis=1, keepdims=True)
        cols, dcols = marks_ref[0], zero
        for k, (a, b) in enumerate(zip(split3(-lse), split3(-delta))):
            cols = jnp.where(lane == 8 + k, a, cols)
            dcols = jnp.where(lane == 8 + k, b, dcols)
        qm.append(jnp.where(mine, q, zero))
        dm.append(jnp.where(mine, do, zero))
        qc.append(jnp.concatenate([qm[h], cols], axis=1))
        dc.append(jnp.concatenate([dm[h], dcols], axis=1))
    qq = jnp.concatenate(qm, axis=0)
    dd = jnp.concatenate(dm, axis=0)
    dq = [0.0, 0.0]
    first = 0
    for g in range(groups):
        S, L = refs[2 * g].shape[0], refs[2 * g].shape[2]
        k, v, km = flat(refs[2 * g], 0, 128), flat(refs[2 * g], 128, 256), flat(refs[2 * g + 1], 0, 128)
        kc = jnp.concatenate([k, km], axis=1)
        vc = jnp.concatenate([v, km], axis=1)
        pts, dss = [], []
        for h in range(2):
            st = dot(kc, qc[h], NT)
            if causal and g == 0:
                st = own_shard_mask(st, nq, 0)
            pt = jnp.exp(st)
            ds = (pt * dot(vc, dc[h], NT)).astype(bf16)
            pts.append(pt.astype(bf16))
            dss.append(ds)
            dq[h] = dq[h] + dot(k, ds, TN)
        dk = dot(jnp.concatenate(dss, axis=1), qq)
        dv = dot(jnp.concatenate(pts, axis=1), dd)
        dkv_ref[first : first + S, 0, :, 0:128] = dk.astype(bf16).reshape(S, L, 128)
        dkv_ref[first : first + S, 0, :, 128:256] = dv.astype(bf16).reshape(S, L, 128)
        first += S
    dq_ref[0] = (jnp.where(lane < 64, dq[0].T, dq[1].T) * 0.125).astype(bf16)


def attn_bwd(q, kvs, kmarks, qmarks, lse, o, do, causal, first, pairs, into=()):
    R, nq, D = q.shape
    each = pl.BlockSpec((1, nq, 128), lambda b, p: (b, 0, first + p))
    once = pl.BlockSpec((1, nq, 128), lambda b, p: (b, 0, 0))
    specs, args = [], []
    for kv, km in zip(kvs, kmarks):
        S, _, L, _ = kv.shape
        specs.append(pl.BlockSpec((S, 1, L, 256), lambda b, p: (0, b, 0, first + p)))
        specs.append(pl.BlockSpec((S, 1, L, 128), lambda b, p: (0, b, 0, 0)))
        args += [kv, km]
    S, L = sum(kv.shape[0] for kv in kvs), kvs[0].shape[2]
    ins = [q, *args, qmarks, lse, o, do]
    return pl.pallas_call(
        functools.partial(bwd_kernel, causal, len(kvs), first),
        grid=(R, pairs),
        in_specs=[each] + specs + [once, once, each, each] + [pl.BlockSpec(memory_space=pl.ANY) for _ in into],
        out_specs=[each, pl.BlockSpec((S, 1, L, 256), lambda b, p: (0, b, 0, first + p))],
        out_shape=[jax.ShapeDtypeStruct((R, nq, D), bf16), jax.ShapeDtypeStruct((S, R, L, 2 * D), bf16)],
        input_output_aliases={len(ins) + k: k for k in range(len(into))},
        compiler_params=pltpu.CompilerParams(vmem_limit_bytes=48 << 20),
        cost_estimate=call_cost(R, nq, S * L, pairs, 5),
        name="attn_bwd",
    )(*ins, *into)


def norm_of(r):
    mean = jnp.mean(r, axis=-1, keepdims=True)
    centered = r - mean
    inv = lax.rsqrt(jnp.mean(centered * centered, axis=-1, keepdims=True) + EPS)
    return centered * inv, inv


def norm_grad(dy, unit, inv, gain):
    f = dy * gain
    return (f - jnp.mean(f, axis=-1, keepdims=True) - unit * jnp.mean(f * unit, axis=-1, keepdims=True)) * inv


def total(x):
    return jnp.sum(x.astype(f32), axis=0, keepdims=True)


def ffn_kernel(
    nb, r2_ref, go_ref, weights_ref, bu_ref, vec_ref,
    out_ref, dr2_ref, do2_ref, grads_ref, gbu_ref, sums_ref,
    h2_ref, unit_ref, inv_ref, low_ref, act_ref, slope_ref, acc_ref, dz_ref,
):
    t, j = pl.program_id(0), pl.program_id(1)
    B = bu_ref.shape[2]
    up_ref, down_ref = weights_ref.at[:, 0:B], weights_ref.at[:, B:]
    g2, s2, bd, g3, s3 = [vec_ref[k : k + 1, :] for k in range(5)]

    @pl.when((t == 0) & (j == 0))
    def _():
        unit, inv = norm_of(r2_ref[...])
        h2 = unit * g2 + s2
        unit_ref[...] = unit
        inv_ref[...] = jnp.broadcast_to(inv, inv_ref.shape)
        low_ref[...] = h2.astype(bf16)
        acc_ref[...] = h2 + bd

    @pl.when(t == 0)
    def _():
        u = dot(low_ref[...], up_ref[...]) + bu_ref[0]
        phi = 0.5 * (1.0 + lax.erf(u * 0.7071067811865476))
        act = (u * phi).astype(bf16)
        act_ref[j] = act
        slope_ref[j] = phi + u * (0.3989422804014327 * jnp.exp(-0.5 * u * u))
        acc_ref[...] += dot(act, down_ref[...])

    @pl.when((t == 0) & (j == nb - 1))
    def _():
        unit, inv = norm_of(acc_ref[...])
        out_ref[...] = (unit * g3 + s3).astype(bf16)
        dy = go_ref[...].astype(f32)
        dr3 = norm_grad(dy, unit, inv, g3)
        dz = dr3.astype(bf16)
        dz_ref[...] = dz
        acc_ref[...] = dr3
        sums_ref[0:1, :] = total(dz)
        sums_ref[1:2, :] = total(dy * unit)
        sums_ref[2:3, :] = total(dy)

    @pl.when(t == 1)
    def _():
        du = (dot(dz_ref[...], down_ref[...], NT) * slope_ref[j]).astype(bf16)
        gbu_ref[0] = total(du)
        grads_ref[:, B:] = dot(act_ref[j], dz_ref[...], TN).astype(bf16)
        grads_ref[:, 0:B] = dot(low_ref[...], du, TN).astype(bf16)
        acc_ref[...] += dot(du, up_ref[...], NT)

    @pl.when((t == 1) & (j == nb - 1))
    def _():
        dy = acc_ref[...]
        dr2 = norm_grad(dy, unit_ref[...], inv_ref[:, 0:1], g2)
        do2 = dr2.astype(bf16)
        dr2_ref[...] = dr2
        do2_ref[...] = do2
        sums_ref[3:4, :] = total(dy * unit_ref[...])
        sums_ref[4:5, :] = total(dy)
        sums_ref[5:6, :] = total(do2)


def ffn(r2, go, weights, bu, vecs):
    T, D = r2.shape
    nb = bu.shape[0]
    B = D
    F = nb * B
    full = lambda a, b: pl.BlockSpec((a, b), lambda t, j: (0, 0))
    shape = jax.ShapeDtypeStruct
    return pl.pallas_call(
        functools.partial(ffn_kernel, nb),
        grid=(2, nb),
        in_specs=[
            full(T, D), full(T, D),
            pl.BlockSpec((D, 2 * B), lambda t, j: (0, j)),
            pl.BlockSpec((1, 1, B), lambda t, j: (j, 0, 0)),
            full(8, D),
        ],
        out_specs=[
            full(T, D), full(T, D), full(T, D),
            pl.BlockSpec((D, 2 * B), lambda t, j: (0, j * t)),
            pl.BlockSpec((1, 1, B), lambda t, j: (j * t, 0, 0)),
            full(8, D),
        ],
        out_shape=[
            shape((T, D), bf16), shape((T, D), f32), shape((T, D), bf16),
            shape((D, 2 * F), bf16), shape((nb, 1, B), f32), shape((8, D), f32),
        ],
        scratch_shapes=[
            pltpu.VMEM((T, D), f32), pltpu.VMEM((T, D), f32), pltpu.VMEM((T, 128), f32), pltpu.VMEM((T, D), bf16),
            pltpu.VMEM((nb, T, B), bf16), pltpu.VMEM((nb, T, B), f32), pltpu.VMEM((T, D), f32), pltpu.VMEM((T, D), bf16),
        ],
        compiler_params=pltpu.CompilerParams(vmem_limit_bytes=56 << 20),
        cost_estimate=pl.CostEstimate(
            flops=12 * T * D * F, bytes_accessed=32 * T * D + 16 * D * F, transcendentals=2 * T * F
        ),
        name="ffn",
    )(r2, go, weights, bu, vecs)


def line_place(k, c):
    return k % c, 128 * (k // c)


def lines_of(tile, first, count):
    c, parts = tile.shape[0], []
    while count:
        y, x = line_place(first, c)
        take = min(count, c - y)
        parts.append(tile[y : y + take, x : x + 128])
        first, count = first + take, count - take
    return parts[0] if len(parts) == 1 else jnp.concatenate(parts, axis=0)


def pack_kernel(nvec, *refs):
    mats, vecs, (bu_ref, ids_ref, out_ref, line_ref) = refs[:8], refs[8 : 8 + nvec], refs[8 + nvec :]
    c, D = mats[0].shape
    at = 0
    for group in ((0,), (1, 2), (3,), (4,), (5, 6), (7,)):
        for p in range(D // 128):
            for i in group:
                out_ref[:, at : at + 128] = mats[i][:, p * 128 : (p + 1) * 128].astype(bf16)
                at += 128
    line_ref[...] = jnp.zeros_like(line_ref)
    for k, r in enumerate(vecs + (bu_ref,)):
        y, x = line_place(k, c)
        line_ref[y : y + 1, x : x + r.shape[1]] = r[...]
    for j in range(ids_ref.shape[0]):
        y, x = line_place(nvec + 1 + j, c)
        line_ref[y : y + 1, x : x + 128] = ids_ref[j : j + 1, :].astype(f32)
    out_ref[:, at:] = line_ref[...].astype(bf16)


def pack_weights(mats, vecs, bu, ids):
    c, D = mats[0].shape
    wide = 128 * (-(-(len(vecs) + 1 + ids.shape[0]) // c))
    return pl.pallas_call(
        functools.partial(pack_kernel, len(vecs)),
        out_shape=jax.ShapeDtypeStruct((c, 8 * D + wide), bf16),
        scratch_shapes=[pltpu.VMEM((c, wide), f32)],
        name="pack_weights",
    )(*mats, *[v.reshape(1, c) for v in vecs], bu.reshape(1, -1), ids)


def pack_ffn_kernel(up_ref, down_ref, out_ref):
    c, D = out_ref.shape[0], down_ref.shape[1]
    for k in range(down_ref.shape[0] // c):
        out_ref[:, 2 * k * D : (2 * k + 1) * D] = up_ref[:, k * D : (k + 1) * D].astype(bf16)
        out_ref[:, (2 * k + 1) * D : (2 * k + 2) * D] = down_ref[k * c : (k + 1) * c, :].astype(bf16)


def pack_ffn(up, down):
    c, F = up.shape
    return pl.pallas_call(pack_ffn_kernel, out_shape=jax.ShapeDtypeStruct((c, 2 * F), bf16), name="pack_ffn")(up, down)


def widen(rows, width, D):
    lane = lax.broadcasted_iota(jnp.int32, rows.shape, 1)
    return jnp.concatenate([jnp.where(lane < width, rows, 0.0), jnp.zeros((rows.shape[0], D - 128), f32)], axis=1)


def spread_kernel(n, nvec, hidden, pairs, line_ref, vec_ref, bu_ref, kv_ref, ids_ref):
    D = vec_ref.shape[1]
    c = D // n
    vec = jnp.zeros((16, D), f32)
    units = jnp.zeros((8, D), f32)
    for d in range(n):
        tile = line_ref[d * c : (d + 1) * c, :].astype(f32)
        rows = jnp.concatenate([lines_of(tile, 0, nvec), jnp.zeros((16 - nvec, 128), f32)], axis=0)
        vec = vec + pltpu.roll(widen(rows, c, D), d * c, axis=1)
        row = jnp.concatenate([lines_of(tile, nvec, 1), jnp.zeros((7, 128), f32)], axis=0)
        ones = [pltpu.roll(row, (128 - k * c) % 128, axis=1)[0:1] for k in range(hidden)]
        ones = jnp.concatenate(ones + [jnp.zeros((8 - hidden, 128), f32)], axis=0)
        units = units + pltpu.roll(widen(ones, c, D), d * c, axis=1)
        ids_ref[d] = lines_of(tile, nvec + 1, ids_ref.shape[1])
    vec_ref[...] = vec
    for k in range(hidden):
        bu_ref[k] = units[k : k + 1]
    kv_ref[...] = jnp.zeros_like(kv_ref)
    for i, k in enumerate(pairs):
        for p in range(D // 128):
            kv_ref[i : i + 1, p * 256 + 128 : (p + 1) * 256] = vec[k : k + 1, p * 128 : (p + 1) * 128]


def spread_lines(lines, n, nvec, hidden, pairs, nids):
    D = lines.shape[0]
    shape = jax.ShapeDtypeStruct
    return pl.pallas_call(
        functools.partial(spread_kernel, n, nvec, hidden, pairs),
        out_shape=[
            shape((16, D), f32), shape((hidden, 1, D), f32), shape((8, 2 * D), f32), shape((n, nids, 128), f32),
        ],
        name="spread_lines",
    )(lines)


def collect_kernel(n, nvec, hidden, *refs):
    vecs, (bu_ref, out_ref, line_ref) = refs[:nvec], refs[nvec:]
    D = vecs[0].shape[1]
    c = D // n
    lane = lax.broadcasted_iota(jnp.int32, (8, 128), 1)
    vec = jnp.concatenate([r[...] for r in vecs] + [jnp.zeros((16 - nvec, D), f32)], axis=0)
    units = jnp.concatenate([bu_ref[k] for k in range(hidden)] + [jnp.zeros((8 - hidden, D), f32)], axis=0)
    line_ref[...] = jnp.zeros_like(line_ref)
    for d in range(n):
        rows = pltpu.roll(vec, (D - d * c) % D, axis=1)[:, 0:128]
        ones = jnp.where(lane < c, pltpu.roll(units, (D - d * c) % D, axis=1)[:, 0:128], 0.0)
        row = sum(pltpu.roll(ones, k * c, axis=1)[k : k + 1] for k in range(hidden))
        for k in range(nvec + 1):
            y, x = line_place(k, c)
            line_ref[d * c + y : d * c + y + 1, x : x + 128] = rows[k : k + 1] if k < nvec else row[0:1]
    out_ref[...] = line_ref[...].astype(bf16)


def collect_lines(vecs, bu, n):
    D = vecs[0].shape[1]
    c = D // n
    wide = 128 * (-(-(len(vecs) + 1) // c))
    return pl.pallas_call(
        functools.partial(collect_kernel, n, len(vecs), bu.shape[0]),
        out_shape=jax.ShapeDtypeStruct((D, wide), bf16),
        scratch_shapes=[pltpu.VMEM((D, wide), f32)],
        name="collect_lines",
    )(*vecs, bu)


def finish_kernel(nvec, cut, mine_ref, other_ref, *outs):
    mats, vecs, bu_ref = outs[:8], outs[8 : 8 + nvec], outs[8 + nvec]
    c, D = mats[0].shape
    full = D // 128
    for ref, groups in (
        (mine_ref, (((0,), 0, full), ((1, 2), cut, full))),
        (other_ref, (((4,), 0, full), ((5, 6), 0, full), ((7,), 0, full), ((3,), 0, full), ((1, 2), 0, cut))),
    ):
        at = 0
        for group, start, stop in groups:
            for p in range(start, stop):
                for i in group:
                    mats[i][:, p * 128 : (p + 1) * 128] = ref[:, at : at + 128].astype(f32)
                    at += 128
    tile = mine_ref[:, D + 256 * (full - cut) :].astype(f32)
    for k in range(nvec + 1):
        y, x = line_place(k, c)
        out = vecs[k] if k < nvec else bu_ref
        out[...] = tile[y : y + 1, x : x + out.shape[1]]


def finish(mine, other, D, nvec, width, cut):
    c = mine.shape[0]
    shape = jax.ShapeDtypeStruct
    out = pl.pallas_call(
        functools.partial(finish_kernel, nvec, cut),
        out_shape=[shape((c, D), f32)] * 8 + [shape((1, c), f32)] * nvec + [shape((1, width), f32)],
        name="finish",
    )(mine, other)
    return out[:8], [v.reshape(-1) for v in out[8:]]


BOTH = ("rows", "seq")


def ring_order(n):
    ny = 2 ** ((n.bit_length() - 1) // 2)
    nz = n // ny
    if ny < 2 or nz < 2:
        return list(range(n))
    order = []
    for z in range(nz):
        ys = list(range(1, ny)) if z % 2 == 0 else list(range(ny - 1, 0, -1))
        order += [z * ny + y for y in ys]
    order += [z * ny for z in range(nz - 1, -1, -1)]
    return order


class Ring:
    def __init__(self, n):
        self.n = n
        self.order = ring_order(n)
        self.up = [(self.order[i], self.order[(i + 1) % n]) for i in range(n)]
        self.down = [(b, a) for a, b in self.up]
        self.near = (n - 1) // 2
        self.far = n - 1 - self.near
        self.offsets = [0]
        for d in range(1, self.far + 1):
            self.offsets.append(-d)
            if d <= self.near:
                self.offsets.append(d)
        place = [0] * n
        for i, s in enumerate(self.order):
            place[s] = i
        me = lax.axis_index("seq")
        every = jnp.arange(n, dtype=jnp.int32)
        spot = jnp.sum(jnp.where(every == me, jnp.asarray(place, jnp.int32), 0))
        at = (spot + jnp.asarray(self.offsets, jnp.int32) + n) % n
        self.owners = jnp.sum(jnp.where(at[:, None] == every, jnp.asarray(self.order, jnp.int32), 0), axis=1)

    def arrange(self, x):
        pick = (self.owners[:, None] == jnp.arange(self.n)).reshape((self.n, self.n) + (1,) * (x.ndim - 1))
        return jnp.sum(jnp.where(pick, x[None], 0), axis=1)

    def hop(self, parts):
        low, high = parts[-2] if len(parts) > 1 else parts[-1], parts[-1]
        fresh = [lax.ppermute(low, "seq", self.up)]
        if len(parts) + 1 < self.n:
            fresh.append(lax.ppermute(high, "seq", self.down))
        return parts + fresh


class RingSum:
    def __init__(self, ring, last):
        self.ring, self.i, self.j = ring, ring.far, ring.near
        self.part = dict(zip(ring.offsets[-len(last) :], last))
        self.held = [self.part[-self.i], self.part[self.j]]

    def join(self, terms):
        self.part.update(zip(self.ring.offsets, terms))

    def add(self, moved, at, left):
        return (moved.astype(f32) + self.part[at].astype(f32)).astype(bf16) if left else moved

    def step(self):
        if self.j >= self.i > 0:
            self.j -= 1
            self.held[1] = self.add(lax.ppermute(self.held[1], "seq", self.ring.up), self.j, self.j)
        if self.i > 0:
            self.i -= 1
            self.held[0] = self.add(lax.ppermute(self.held[0], "seq", self.ring.down), -self.i, self.i)

    def finish(self):
        while self.i or self.j:
            self.step()
        return sum((h.astype(f32) for h in self.held), self.part[0].astype(f32))


class Halving:
    def __init__(self, rows, seq, x, early=None):
        self.rows, self.bits = rows, rows.bit_length() - 1
        self.steps = list(range(self.bits))
        self.steps.insert(self.bits if early is None else min(early, self.bits), "seq")
        self.left, self.open = self.bits, False
        self.held = [x.reshape((2,) * self.bits + (seq, -1, x.shape[-1]))]

    def settle(self, kind):
        x = self.held[0]
        if self.open:
            self.open = False
            return jnp.sum(x.astype(f32), axis=self.left).astype(kind)
        return x.astype(kind)

    def step(self):
        x, b = self.settle(bf16), self.steps.pop(0)
        if b == "seq":
            self.held, self.open = [lax.all_to_all(x, "seq", self.left, self.left)], True
            return
        self.left -= 1
        mine = (lax.axis_index("rows") >> b) & 1
        keep = lax.dynamic_index_in_dim(x, mine, self.left, keepdims=False)
        send = lax.dynamic_index_in_dim(x, 1 - mine, self.left, keepdims=False)
        got = lax.ppermute(send, "rows", [(j, j ^ (1 << b)) for j in range(self.rows)])
        self.held = [(keep.astype(f32) + got.astype(f32)).astype(bf16)]

    def finish(self):
        while self.steps:
            self.step()
        return self.settle(f32)


def slot(values, *moving):
    held = [h for m in moving for h in m.held]
    out = list(lax.optimization_barrier(tuple(values) + tuple(held)))
    for m in reversed(moving):
        m.held = out[-len(m.held) :]
        del out[-len(m.held) :]
    return out


def together(*xs):
    return lax.optimization_barrier(xs)


def norm(resid, gain, shift):
    mean = jnp.mean(resid, axis=-1, keepdims=True)
    centered = resid - mean
    inv = lax.rsqrt(jnp.mean(centered * centered, axis=-1, keepdims=True) + EPS)
    unit = centered * inv
    return unit * gain + shift, unit, inv


def norm_back(dy, unit, inv, gain):
    f = dy * gain
    mean = jnp.mean(f, axis=-1, keepdims=True)
    cross = jnp.mean(f * unit, axis=-1, keepdims=True)
    return (f - mean - unit * cross) * inv, jnp.sum(dy * unit, axis=0), jnp.sum(dy, axis=0)


def colsum(x):
    return jnp.sum(x.astype(f32), axis=0)


def key_marks(seg, hidden):
    lane = jnp.arange(128)
    marks = jnp.where(lane < 3, jnp.where(seg[..., None] == lane, 0.0, BIG), 0.0)
    if hidden is not None:
        marks = jnp.where(lane == 3, jnp.where(hidden[..., None], BIG, 0.0), marks)
    return jnp.where((lane >= 8) & (lane <= 10), 1.0, marks).astype(bf16)


def query_marks(seg):
    lane = jnp.arange(128)
    return ((seg[..., None] == lane) | (lane == 3)).astype(bf16)


def row_major(x):
    return with_layout_constraint(x, Layout(tuple(range(x.ndim))))


def layer(nrows, nseq, *args):
    (
        target, memory, target_seg, memory_seg, grad_output,
        self_query, self_qbias, self_key, self_value, self_vbias, self_out, self_obias, norm1_gain, norm1_shift,
        cross_query, cross_qbias, cross_key, cross_value, cross_vbias, cross_out, cross_obias, norm2_gain, norm2_shift,
        ffn_up, ffn_ubias, ffn_down, ffn_dbias, norm3_gain, norm3_shift,
    ) = args
    n = nrows * nseq
    R, L, D = target.shape
    c = self_query.shape[0]
    F = ffn_up.shape[1]
    m = F // D
    ring = Ring(nseq)

    mats = (self_query, self_key, self_value, self_out, cross_query, cross_key, cross_value, cross_out)
    vecs = (
        self_qbias, self_vbias, self_obias, norm1_gain, norm1_shift, cross_qbias, cross_vbias, cross_obias,
        norm2_gain, norm2_shift, ffn_dbias, norm3_gain, norm3_shift,
    )
    nvec = len(vecs)
    ids = jnp.concatenate([target_seg, memory_seg], axis=0).reshape(-1, 128)
    pack = pack_weights(mats, vecs, ffn_ubias, ids)
    everything = lax.all_gather(pack, BOTH, axis=0, tiled=True)
    x = target.reshape(R * L, D)
    parts = [row_major(x)]
    while len(parts) < nseq:
        parts = ring.hop(parts)
    pack_f = pack_ffn(ffn_up.reshape(c, n, m, c).transpose(0, 2, 1, 3).reshape(c, F), ffn_down)
    X = row_major(jnp.concatenate(parts, axis=0))
    everything, pack_f, memory, X = together(everything, pack_f, memory, X)
    wanted = ring.hop([row_major(memory.reshape(R * L, D))])
    wffn = lax.all_gather(pack_f, BOTH, axis=0, tiled=True)
    wq, wkv, wo, cq, ckv, co = [
        everything[:, a * D : b * D] for a, b in ((0, 1), (1, 3), (3, 4), (4, 5), (5, 7), (7, 8))
    ]
    vec, bu, pairs, segs = spread_lines(everything[:, 8 * D :], n, nvec, m, (1, 6), ids.shape[0])
    bq, _, bo, g1, s1, bcq, _, bco, g2, s2, bd, g3, s3 = [vec[k : k + 1] for k in range(nvec)]
    bkv, bckv = pairs[0:1], pairs[1:2]

    segs = segs.reshape(nrows, nseq, 2 * R, L)
    mine = (jnp.arange(nrows) == lax.axis_index("rows")).reshape(nrows, 1, 1, 1)
    segs = ring.arrange(jnp.sum(jnp.where(mine, segs, 0.0), axis=0).astype(jnp.int32))
    hidden = (ring.owners > lax.axis_index("seq"))[:, None, None]
    half = (nseq + 1) // 2
    self_marks = [key_marks(segs[:, :R], hidden)]
    cross_marks = [key_marks(s, None) for s in (segs[:half, R:], segs[half:, R:])]
    marks = query_marks(target_seg)

    def rows(t):
        return t.reshape(R, -1, t.shape[-1])

    def pile(parts):
        return row_major(jnp.concatenate(parts, axis=0))

    def project(parts, w, b):
        return (dot(parts, w) + b).astype(bf16).reshape(-1, R, L, 2 * D)

    def pieces(t):
        return list(t.reshape(-1, R, L, D))

    KV = [project(X, wkv, bkv)]
    Q = rows((dot(x, wq) + bq).astype(bf16))
    Q, KV[0], *wanted = together(Q, KV[0], *wanted)
    wanted = ring.hop(wanted)
    A1, lse1 = attn_fwd(Q, KV, self_marks, marks, True)
    A1, lse1, *wanted = together(A1, lse1, *wanted)
    wanted = ring.hop(wanted)
    a1 = A1.reshape(R * L, D).astype(bf16)
    R1 = x.astype(f32) + dot(a1, wo) + bo
    H1, N1, i1 = norm(R1, g1, s1)
    h1 = H1.astype(bf16)
    CQ = rows((dot(h1, cq) + bcq).astype(bf16))
    while len(wanted) < half:
        wanted = ring.hop(wanted)
    Ms = [pile(wanted[:half])]
    CKV = [project(Ms[0], ckv, bckv)]
    CQ, CKV[0], *wanted = together(CQ, CKV[0], *wanted)
    while len(wanted) < nseq:
        wanted = ring.hop(wanted)
    Ms.append(pile(wanted[half:]))
    CKV.append(project(Ms[1], ckv, bckv))
    A2, lse2 = attn_fwd(CQ, CKV, cross_marks, marks, False)
    a2 = A2.reshape(R * L, D).astype(bf16)
    R2 = H1 + dot(a2, co) + bco

    knobs = jnp.concatenate([vec[8:13], jnp.zeros((3, D), f32)], axis=0)
    output, dR2, dO2, w_ffn, dbu, sums = ffn(R2, grad_output.reshape(R * L, D), wffn, bu, knobs)
    output = rows(output)
    gbd, dg3, ds3, dg2, ds2, gbco = [sums[k : k + 1] for k in range(6)]

    def halved(w, early=None):
        return Halving(nrows, nseq, w, early)

    def scattered(w):
        return lax.psum_scatter(w, BOTH, scatter_dimension=0, tiled=True)

    npair = D // 128
    cuts = (0, npair // 3, 2 * npair // 3, npair)
    near = half * R * L
    g_ffn = scattered(w_ffn)
    w_co = dot(a2, dO2, TN).astype(bf16)
    dA2 = rows(dot(dO2, co, NT).astype(bf16))
    dA2, w_co = slot([dA2, w_co])
    dCQ, dCKV = slot(attn_bwd(CQ, CKV, cross_marks, marks, lse2, A2, dA2, False, 0, npair))
    g = dCKV.reshape(-1, 2 * D)
    dM = dot(g, ckv, NT).astype(bf16)
    dCQ = dCQ.reshape(R * L, D)
    dM, dCQ, g = slot([dM, dCQ, g])
    to_memory = RingSum(ring, pieces(dM))
    to_memory.step()
    w_ckv = (dot(Ms[0], g[:near], TN) + dot(Ms[1], g[near:], TN)).astype(bf16)
    dCQ, w_ckv = slot([dCQ, w_ckv])
    w_cq = dot(h1, dCQ, TN).astype(bf16)
    dH1 = dR2 + dot(dCQ, cq, NT)
    dR1, dg1, ds1 = norm_back(dH1, N1, i1, g1)
    (dR1,) = slot([dR1], to_memory)
    to_memory.step()
    dO1 = dR1.astype(bf16)
    dA1 = rows(dot(dO1, wo, NT).astype(bf16))
    w_o = dot(a1, dO1, TN).astype(bf16)
    dA1, w_o, w_cq = slot([dA1, w_o, w_cq])
    own = (Q, KV, self_marks, marks, lse1, A1, dA1, True)
    into = ()
    for k in range(3):
        if k:
            to_memory.step()
        at, count = cuts[k], cuts[k + 1] - cuts[k]
        into = attn_bwd(*own, at, count, into)
        if k == 0:
            w_kv1 = dot(X, into[1].reshape(-1, 2 * D)[:, : 256 * count], TN).astype(bf16)
            others = jnp.concatenate([w_cq, w_ckv, w_co, w_o, w_kv1], axis=1)
            *into, others = slot([*into, others], to_memory)
        elif k == 1:
            *into, others, g_ffn = slot([*into, others, g_ffn], to_memory)
            others = scattered(others)
        else:
            into = slot(into, to_memory)
    to_memory.step()
    dQ, dKV = into
    g = dKV.reshape(-1, 2 * D)
    dQ = dQ.reshape(R * L, D)
    dX = dot(g, wkv, NT).astype(bf16)
    g, dQ, dX = slot([g, dQ, dX])
    to_target = RingSum(ring, pieces(dX))
    to_target.step()
    w_kv2 = dot(X, g[:, 256 * cuts[1] :], TN).astype(bf16)
    w_q = dot(x, dQ, TN).astype(bf16)
    vec_sums = [
        v.reshape(1, D)
        for v in (
            colsum(dQ), colsum(dA1.reshape(R * L, D)), colsum(dO1), dg1, ds1,
            colsum(dCQ), colsum(dA2.reshape(R * L, D)), gbco, dg2, ds2, gbd, dg3, ds3,
        )
    ]
    late = jnp.concatenate([w_q, w_kv2, collect_lines(vec_sums, dbu, n)], axis=1)
    (late,) = slot([late], to_target)
    late = halved(late)
    late.step()
    to_target.step()
    late.step()
    to_target.step()
    late.step()
    target_gradient = (rows(dR1 + dot(dQ, wq, NT)) + rows(to_target.finish())).astype(bf16)
    memory_gradient = to_memory.finish().astype(bf16).reshape(R, L, D)
    sides = g_ffn.reshape(c, m, 2, D)
    g_up = sides[:, :, 0].reshape(c, m, n, c).transpose(0, 2, 1, 3).reshape(c, F).astype(f32)
    g_down = sides[:, :, 1].transpose(1, 0, 2).reshape(m * c, D).astype(f32)
    grads, small = finish(late.finish(), others, D, nvec, m * c, cuts[1])
    gq, gk, gv, go, gcq, gck, gcv, gco = grads
    (gbq, gbv, gbo, gg1, gs1, gbcq, gbcv, gbco, gg2, gs2, gbd, gg3, gs3, gbu) = small
    return (
        output, target_gradient, memory_gradient,
        gq, gbq, gk, gv, gbv, go, gbo, gg1, gs1,
        gcq, gbcq, gck, gcv, gbcv, gco, gbco, gg2, gs2,
        g_up, gbu, g_down, gbd, gg3, gs3,
    )


def solution(mesh):
    act, ids, mat, vec = P("rows", "seq", None), P("rows", "seq"), P(BOTH, None), P(BOTH)
    ins = (
        act, act, ids, ids, act,
        mat, vec, mat, mat, vec, mat, vec, vec, vec,
        mat, vec, mat, mat, vec, mat, vec, vec, vec,
        mat, vec, mat, vec, vec, vec,
    )
    outs = (
        act, act, act,
        mat, vec, mat, mat, vec, mat, vec, vec, vec,
        mat, vec, mat, mat, vec, mat, vec, vec, vec,
        mat, vec, mat, vec, vec, vec,
    )
    run = functools.partial(layer, mesh.shape["rows"], mesh.shape["seq"])
    return jax.shard_map(run, mesh=mesh, in_specs=ins, out_specs=outs, check_vma=False)
```

```python
import functools

import jax
import jax.numpy as jnp
from jax import lax
from jax.experimental import pallas as pl
from jax.experimental.pallas import tpu as pltpu
from jax.experimental.layout import Layout, with_layout_constraint
from jax.sharding import PartitionSpec as P

f32 = jnp.float32
bf16 = jnp.bfloat16
EPS = 1e-05
BIG = -1e30
NT = (((1,), (1,)), ((), ()))
TN = (((0,), (0,)), ((), ()))


def dot(a, b, dims=(((1,), (0,)), ((), ()))):
    return lax.dot_general(a, b, dims, preferred_element_type=f32)


def own_shard_mask(s, nq, keys):
    ki = lax.broadcasted_iota(jnp.int32, s.shape, keys)
    qi = lax.broadcasted_iota(jnp.int32, s.shape, 1 - keys)
    return jnp.where((ki >= nq) | (ki <= qi), s, BIG)


def flat(ref, lo, hi):
    return ref[:, 0, :, lo:hi].reshape(ref.shape[0] * ref.shape[2], hi - lo)


def fwd_kernel(causal, groups, q_ref, *refs):
    marks_ref, o_ref, lse_ref = refs[2 * groups :]
    p = pl.program_id(1)
    nq = q_ref.shape[1]
    lane = lax.broadcasted_iota(jnp.int32, (nq, 128), 1)
    q = q_ref[0] * jnp.asarray(0.125, bf16)
    zero = jnp.zeros_like(q)
    outs, lses = [], []
    for h in range(2):
        mine = (lane < 64) if h == 0 else (lane >= 64)
        qc = jnp.concatenate([jnp.where(mine, q, zero), marks_ref[0]], axis=1)
        ss, m = [], None
        for g in range(groups):
            s = dot(qc, jnp.concatenate([flat(refs[2 * g], 0, 128), flat(refs[2 * g + 1], 0, 128)], axis=1), NT)
            if causal and g == 0:
                s = own_shard_mask(s, nq, 1)
            ss.append(s)
            mc = jnp.max(s, axis=1, keepdims=True)
            m = mc if m is None else jnp.maximum(m, mc)
        l, o = 0.0, 0.0
        for g in range(groups):
            e = jnp.exp(ss[g] - m)
            l = l + jnp.sum(e, axis=1, keepdims=True)
            o = o + dot(e.astype(bf16), flat(refs[2 * g], 128, 256))
        outs.append(o / l)
        lses.append(m + jnp.log(l))
    o_ref[0] = jnp.where(lane < 64, outs[0], outs[1])

    @pl.when(p == 0)
    def _():
        lse_ref[...] = jnp.zeros_like(lse_ref)

    lse_ref[0] = jnp.where(lane == 2 * p, lses[0], jnp.where(lane == 2 * p + 1, lses[1], lse_ref[0]))


def call_cost(R, nq, nk, npair, dots):
    return pl.CostEstimate(
        flops=R * npair * 4 * dots * nq * nk * 256,
        bytes_accessed=R * npair * nk * 512,
        transcendentals=R * npair * 2 * nq * nk,
    )


def key_specs(kvs, kmarks):
    specs, args = [], []
    for kv, km in zip(kvs, kmarks):
        S, _, L, _ = kv.shape
        specs.append(pl.BlockSpec((S, 1, L, 256), lambda b, p: (0, b, 0, p)))
        specs.append(pl.BlockSpec((S, 1, L, 128), lambda b, p: (0, b, 0, 0)))
        args += [kv, km]
    return specs, args


def attn_fwd(q, kvs, kmarks, qmarks, causal):
    R, nq, D = q.shape
    npair = D // 128
    each = pl.BlockSpec((1, nq, 128), lambda b, p: (b, 0, p))
    once = pl.BlockSpec((1, nq, 128), lambda b, p: (b, 0, 0))
    specs, args = key_specs(kvs, kmarks)
    nk = sum(kv.shape[0] * kv.shape[2] for kv in kvs)
    return pl.pallas_call(
        functools.partial(fwd_kernel, causal, len(kvs)),
        grid=(R, npair),
        in_specs=[each] + specs + [once],
        out_specs=[each, once],
        out_shape=[jax.ShapeDtypeStruct((R, nq, D), f32), jax.ShapeDtypeStruct((R, nq, 128), f32)],
        compiler_params=pltpu.CompilerParams(vmem_limit_bytes=40 << 20),
        cost_estimate=call_cost(R, nq, nk, npair, 3),
        name="attn_fwd",
    )(q, *args, qmarks)


def split3(x):
    a = x.astype(bf16)
    r = x - a.astype(f32)
    b = r.astype(bf16)
    return a, b, (r - b.astype(f32)).astype(bf16)


def bwd_kernel(causal, groups, first_pair, q_ref, *refs):
    marks_ref, lse_ref, o_ref, do_ref = refs[2 * groups : 2 * groups + 4]
    dq_ref, dkv_ref = refs[-2:]
    p = first_pair + pl.program_id(1)
    nq = q_ref.shape[1]
    lane = lax.broadcasted_iota(jnp.int32, (nq, 128), 1)
    q = q_ref[0] * jnp.asarray(0.125, bf16)
    do = do_ref[0]
    zero = jnp.zeros_like(q)
    prod = do.astype(f32) * o_ref[0]
    qc, dc, qm, dm = [], [], [], []
    for h in range(2):
        mine = (lane < 64) if h == 0 else (lane >= 64)
        lse = jnp.sum(jnp.where(lane == 2 * p + h, lse_ref[0], 0.0), axis=1, keepdims=True)
        delta = jnp.sum(jnp.where(mine, prod, 0.0), axis=1, keepdims=True)
        cols, dcols = marks_ref[0], zero
        for k, (a, b) in enumerate(zip(split3(-lse), split3(-delta))):
            cols = jnp.where(lane == 8 + k, a, cols)
            dcols = jnp.where(lane == 8 + k, b, dcols)
        qm.append(jnp.where(mine, q, zero))
        dm.append(jnp.where(mine, do, zero))
        qc.append(jnp.concatenate([qm[h], cols], axis=1))
        dc.append(jnp.concatenate([dm[h], dcols], axis=1))
    qq = jnp.concatenate(qm, axis=0)
    dd = jnp.concatenate(dm, axis=0)
    dq = [0.0, 0.0]
    first = 0
    for g in range(groups):
        S, L = refs[2 * g].shape[0], refs[2 * g].shape[2]
        k, v, km = flat(refs[2 * g], 0, 128), flat(refs[2 * g], 128, 256), flat(refs[2 * g + 1], 0, 128)
        kc = jnp.concatenate([k, km], axis=1)
        vc = jnp.concatenate([v, km], axis=1)
        pts, dss = [], []
        for h in range(2):
            st = dot(kc, qc[h], NT)
            if causal and g == 0:
                st = own_shard_mask(st, nq, 0)
            pt = jnp.exp(st)
            ds = (pt * dot(vc, dc[h], NT)).astype(bf16)
            pts.append(pt.astype(bf16))
            dss.append(ds)
            dq[h] = dq[h] + dot(k, ds, TN)
        dk = dot(jnp.concatenate(dss, axis=1), qq)
        dv = dot(jnp.concatenate(pts, axis=1), dd)
        dkv_ref[first : first + S, 0, :, 0:128] = dk.astype(bf16).reshape(S, L, 128)
        dkv_ref[first : first + S, 0, :, 128:256] = dv.astype(bf16).reshape(S, L, 128)
        first += S
    dq_ref[0] = (jnp.where(lane < 64, dq[0].T, dq[1].T) * 0.125).astype(bf16)


def attn_bwd(q, kvs, kmarks, qmarks, lse, o, do, causal, first, pairs, into=()):
    R, nq, D = q.shape
    each = pl.BlockSpec((1, nq, 128), lambda b, p: (b, 0, first + p))
    once = pl.BlockSpec((1, nq, 128), lambda b, p: (b, 0, 0))
    specs, args = [], []
    for kv, km in zip(kvs, kmarks):
        S, _, L, _ = kv.shape
        specs.append(pl.BlockSpec((S, 1, L, 256), lambda b, p: (0, b, 0, first + p)))
        specs.append(pl.BlockSpec((S, 1, L, 128), lambda b, p: (0, b, 0, 0)))
        args += [kv, km]
    S, L = sum(kv.shape[0] for kv in kvs), kvs[0].shape[2]
    ins = [q, *args, qmarks, lse, o, do]
    return pl.pallas_call(
        functools.partial(bwd_kernel, causal, len(kvs), first),
        grid=(R, pairs),
        in_specs=[each] + specs + [once, once, each, each] + [pl.BlockSpec(memory_space=pl.ANY) for _ in into],
        out_specs=[each, pl.BlockSpec((S, 1, L, 256), lambda b, p: (0, b, 0, first + p))],
        out_shape=[jax.ShapeDtypeStruct((R, nq, D), bf16), jax.ShapeDtypeStruct((S, R, L, 2 * D), bf16)],
        input_output_aliases={len(ins) + k: k for k in range(len(into))},
        compiler_params=pltpu.CompilerParams(vmem_limit_bytes=48 << 20),
        cost_estimate=call_cost(R, nq, S * L, pairs, 5),
        name="attn_bwd",
    )(*ins, *into)


def norm_of(r):
    mean = jnp.mean(r, axis=-1, keepdims=True)
    centered = r - mean
    inv = lax.rsqrt(jnp.mean(centered * centered, axis=-1, keepdims=True) + EPS)
    return centered * inv, inv


def norm_grad(dy, unit, inv, gain):
    f = dy * gain
    return (f - jnp.mean(f, axis=-1, keepdims=True) - unit * jnp.mean(f * unit, axis=-1, keepdims=True)) * inv


def total(x):
    return jnp.sum(x.astype(f32), axis=0, keepdims=True)


def ffn_kernel(
    nb, r2_ref, go_ref, weights_ref, bu_ref, vec_ref,
    out_ref, dr2_ref, do2_ref, grads_ref, gbu_ref, sums_ref,
    h2_ref, unit_ref, inv_ref, low_ref, act_ref, slope_ref, acc_ref, dz_ref,
):
    t, j = pl.program_id(0), pl.program_id(1)
    B = bu_ref.shape[2]
    up_ref, down_ref = weights_ref.at[:, 0:B], weights_ref.at[:, B:]
    g2, s2, bd, g3, s3 = [vec_ref[k : k + 1, :] for k in range(5)]

    @pl.when((t == 0) & (j == 0))
    def _():
        unit, inv = norm_of(r2_ref[...])
        h2 = unit * g2 + s2
        unit_ref[...] = unit
        inv_ref[...] = jnp.broadcast_to(inv, inv_ref.shape)
        low_ref[...] = h2.astype(bf16)
        acc_ref[...] = h2 + bd

    @pl.when(t == 0)
    def _():
        u = dot(low_ref[...], up_ref[...]) + bu_ref[0]
        phi = 0.5 * (1.0 + lax.erf(u * 0.7071067811865476))
        act = (u * phi).astype(bf16)
        act_ref[j] = act
        slope_ref[j] = phi + u * (0.3989422804014327 * jnp.exp(-0.5 * u * u))
        acc_ref[...] += dot(act, down_ref[...])

    @pl.when((t == 0) & (j == nb - 1))
    def _():
        unit, inv = norm_of(acc_ref[...])
        out_ref[...] = (unit * g3 + s3).astype(bf16)
        dy = go_ref[...].astype(f32)
        dr3 = norm_grad(dy, unit, inv, g3)
        dz = dr3.astype(bf16)
        dz_ref[...] = dz
        acc_ref[...] = dr3
        sums_ref[0:1, :] = total(dz)
        sums_ref[1:2, :] = total(dy * unit)
        sums_ref[2:3, :] = total(dy)

    @pl.when(t == 1)
    def _():
        du = (dot(dz_ref[...], down_ref[...], NT) * slope_ref[j]).astype(bf16)
        gbu_ref[0] = total(du)
        grads_ref[:, B:] = dot(act_ref[j], dz_ref[...], TN).astype(bf16)
        grads_ref[:, 0:B] = dot(low_ref[...], du, TN).astype(bf16)
        acc_ref[...] += dot(du, up_ref[...], NT)

    @pl.when((t == 1) & (j == nb - 1))
    def _():
        dy = acc_ref[...]
        dr2 = norm_grad(dy, unit_ref[...], inv_ref[:, 0:1], g2)
        do2 = dr2.astype(bf16)
        dr2_ref[...] = dr2
        do2_ref[...] = do2
        sums_ref[3:4, :] = total(dy * unit_ref[...])
        sums_ref[4:5, :] = total(dy)
        sums_ref[5:6, :] = total(do2)


def ffn(r2, go, weights, bu, vecs):
    T, D = r2.shape
    nb = bu.shape[0]
    B = D
    F = nb * B
    full = lambda a, b: pl.BlockSpec((a, b), lambda t, j: (0, 0))
    shape = jax.ShapeDtypeStruct
    return pl.pallas_call(
        functools.partial(ffn_kernel, nb),
        grid=(2, nb),
        in_specs=[
            full(T, D), full(T, D),
            pl.BlockSpec((D, 2 * B), lambda t, j: (0, j)),
            pl.BlockSpec((1, 1, B), lambda t, j: (j, 0, 0)),
            full(8, D),
        ],
        out_specs=[
            full(T, D), full(T, D), full(T, D),
            pl.BlockSpec((D, 2 * B), lambda t, j: (0, j * t)),
            pl.BlockSpec((1, 1, B), lambda t, j: (j * t, 0, 0)),
            full(8, D),
        ],
        out_shape=[
            shape((T, D), bf16), shape((T, D), f32), shape((T, D), bf16),
            shape((D, 2 * F), bf16), shape((nb, 1, B), f32), shape((8, D), f32),
        ],
        scratch_shapes=[
            pltpu.VMEM((T, D), f32), pltpu.VMEM((T, D), f32), pltpu.VMEM((T, 128), f32), pltpu.VMEM((T, D), bf16),
            pltpu.VMEM((nb, T, B), bf16), pltpu.VMEM((nb, T, B), f32), pltpu.VMEM((T, D), f32), pltpu.VMEM((T, D), bf16),
        ],
        compiler_params=pltpu.CompilerParams(vmem_limit_bytes=56 << 20),
        cost_estimate=pl.CostEstimate(
            flops=12 * T * D * F, bytes_accessed=32 * T * D + 16 * D * F, transcendentals=2 * T * F
        ),
        name="ffn",
    )(r2, go, weights, bu, vecs)


def line_place(k, c):
    return k % c, 128 * (k // c)


def lines_of(tile, first, count):
    c, parts = tile.shape[0], []
    while count:
        y, x = line_place(first, c)
        take = min(count, c - y)
        parts.append(tile[y : y + take, x : x + 128])
        first, count = first + take, count - take
    return parts[0] if len(parts) == 1 else jnp.concatenate(parts, axis=0)


def pack_kernel(nvec, *refs):
    mats, vecs, (bu_ref, ids_ref, out_ref, line_ref) = refs[:8], refs[8 : 8 + nvec], refs[8 + nvec :]
    c, D = mats[0].shape
    at = 0
    for group in ((0,), (1, 2), (3,), (4,), (5, 6), (7,)):
        for p in range(D // 128):
            for i in group:
                out_ref[:, at : at + 128] = mats[i][:, p * 128 : (p + 1) * 128].astype(bf16)
                at += 128
    line_ref[...] = jnp.zeros_like(line_ref)
    for k, r in enumerate(vecs + (bu_ref,)):
        y, x = line_place(k, c)
        line_ref[y : y + 1, x : x + r.shape[1]] = r[...]
    for j in range(ids_ref.shape[0]):
        y, x = line_place(nvec + 1 + j, c)
        line_ref[y : y + 1, x : x + 128] = ids_ref[j : j + 1, :].astype(f32)
    out_ref[:, at:] = line_ref[...].astype(bf16)


def pack_weights(mats, vecs, bu, ids):
    c, D = mats[0].shape
    wide = 128 * (-(-(len(vecs) + 1 + ids.shape[0]) // c))
    return pl.pallas_call(
        functools.partial(pack_kernel, len(vecs)),
        out_shape=jax.ShapeDtypeStruct((c, 8 * D + wide), bf16),
        scratch_shapes=[pltpu.VMEM((c, wide), f32)],
        name="pack_weights",
    )(*mats, *[v.reshape(1, c) for v in vecs], bu.reshape(1, -1), ids)


def pack_ffn_kernel(up_ref, down_ref, out_ref):
    c, D = out_ref.shape[0], down_ref.shape[1]
    for k in range(down_ref.shape[0] // c):
        out_ref[:, 2 * k * D : (2 * k + 1) * D] = up_ref[:, k * D : (k + 1) * D].astype(bf16)
        out_ref[:, (2 * k + 1) * D : (2 * k + 2) * D] = down_ref[k * c : (k + 1) * c, :].astype(bf16)


def pack_ffn(up, down):
    c, F = up.shape
    return pl.pallas_call(pack_ffn_kernel, out_shape=jax.ShapeDtypeStruct((c, 2 * F), bf16), name="pack_ffn")(up, down)


def widen(rows, width, D):
    lane = lax.broadcasted_iota(jnp.int32, rows.shape, 1)
    return jnp.concatenate([jnp.where(lane < width, rows, 0.0), jnp.zeros((rows.shape[0], D - 128), f32)], axis=1)


def spread_kernel(n, nvec, hidden, pairs, line_ref, vec_ref, bu_ref, kv_ref, ids_ref):
    D = vec_ref.shape[1]
    c = D // n
    vec = jnp.zeros((16, D), f32)
    units = jnp.zeros((8, D), f32)
    for d in range(n):
        tile = line_ref[d * c : (d + 1) * c, :].astype(f32)
        rows = jnp.concatenate([lines_of(tile, 0, nvec), jnp.zeros((16 - nvec, 128), f32)], axis=0)
        vec = vec + pltpu.roll(widen(rows, c, D), d * c, axis=1)
        row = jnp.concatenate([lines_of(tile, nvec, 1), jnp.zeros((7, 128), f32)], axis=0)
        ones = [pltpu.roll(row, (128 - k * c) % 128, axis=1)[0:1] for k in range(hidden)]
        ones = jnp.concatenate(ones + [jnp.zeros((8 - hidden, 128), f32)], axis=0)
        units = units + pltpu.roll(widen(ones, c, D), d * c, axis=1)
        ids_ref[d] = lines_of(tile, nvec + 1, ids_ref.shape[1])
    vec_ref[...] = vec
    for k in range(hidden):
        bu_ref[k] = units[k : k + 1]
    kv_ref[...] = jnp.zeros_like(kv_ref)
    for i, k in enumerate(pairs):
        for p in range(D // 128):
            kv_ref[i : i + 1, p * 256 + 128 : (p + 1) * 256] = vec[k : k + 1, p * 128 : (p + 1) * 128]


def spread_lines(lines, n, nvec, hidden, pairs, nids):
    D = lines.shape[0]
    shape = jax.ShapeDtypeStruct
    return pl.pallas_call(
        functools.partial(spread_kernel, n, nvec, hidden, pairs),
        out_shape=[
            shape((16, D), f32), shape((hidden, 1, D), f32), shape((8, 2 * D), f32), shape((n, nids, 128), f32),
        ],
        name="spread_lines",
    )(lines)


def collect_kernel(n, nvec, hidden, *refs):
    vecs, (bu_ref, out_ref, line_ref) = refs[:nvec], refs[nvec:]
    D = vecs[0].shape[1]
    c = D // n
    lane = lax.broadcasted_iota(jnp.int32, (8, 128), 1)
    vec = jnp.concatenate([r[...] for r in vecs] + [jnp.zeros((16 - nvec, D), f32)], axis=0)
    units = jnp.concatenate([bu_ref[k] for k in range(hidden)] + [jnp.zeros((8 - hidden, D), f32)], axis=0)
    line_ref[...] = jnp.zeros_like(line_ref)
    for d in range(n):
        rows = pltpu.roll(vec, (D - d * c) % D, axis=1)[:, 0:128]
        ones = jnp.where(lane < c, pltpu.roll(units, (D - d * c) % D, axis=1)[:, 0:128], 0.0)
        row = sum(pltpu.roll(ones, k * c, axis=1)[k : k + 1] for k in range(hidden))
        for k in range(nvec + 1):
            y, x = line_place(k, c)
            line_ref[d * c + y : d * c + y + 1, x : x + 128] = rows[k : k + 1] if k < nvec else row[0:1]
    out_ref[...] = line_ref[...].astype(bf16)


def collect_lines(vecs, bu, n):
    D = vecs[0].shape[1]
    c = D // n
    wide = 128 * (-(-(len(vecs) + 1) // c))
    return pl.pallas_call(
        functools.partial(collect_kernel, n, len(vecs), bu.shape[0]),
        out_shape=jax.ShapeDtypeStruct((D, wide), bf16),
        scratch_shapes=[pltpu.VMEM((D, wide), f32)],
        name="collect_lines",
    )(*vecs, bu)


def finish_kernel(nvec, cut, mine_ref, other_ref, *outs):
    mats, vecs, bu_ref = outs[:8], outs[8 : 8 + nvec], outs[8 + nvec]
    c, D = mats[0].shape
    full = D // 128
    for ref, groups in (
        (mine_ref, (((0,), 0, full), ((1, 2), cut, full))),
        (other_ref, (((4,), 0, full), ((5, 6), 0, full), ((7,), 0, full), ((3,), 0, full), ((1, 2), 0, cut))),
    ):
        at = 0
        for group, start, stop in groups:
            for p in range(start, stop):
                for i in group:
                    mats[i][:, p * 128 : (p + 1) * 128] = ref[:, at : at + 128].astype(f32)
                    at += 128
    tile = mine_ref[:, D + 256 * (full - cut) :].astype(f32)
    for k in range(nvec + 1):
        y, x = line_place(k, c)
        out = vecs[k] if k < nvec else bu_ref
        out[...] = tile[y : y + 1, x : x + out.shape[1]]


def finish(mine, other, D, nvec, width, cut):
    c = mine.shape[0]
    shape = jax.ShapeDtypeStruct
    out = pl.pallas_call(
        functools.partial(finish_kernel, nvec, cut),
        out_shape=[shape((c, D), f32)] * 8 + [shape((1, c), f32)] * nvec + [shape((1, width), f32)],
        name="finish",
    )(mine, other)
    return out[:8], [v.reshape(-1) for v in out[8:]]


BOTH = ("rows", "seq")


def ring_order(n):
    ny = 2 ** ((n.bit_length() - 1) // 2)
    nz = n // ny
    if ny < 2 or nz < 2:
        return list(range(n))
    order = []
    for z in range(nz):
        ys = list(range(1, ny)) if z % 2 == 0 else list(range(ny - 1, 0, -1))
        order += [z * ny + y for y in ys]
    order += [z * ny for z in range(nz - 1, -1, -1)]
    return order


class Ring:
    def __init__(self, n):
        self.n = n
        self.order = ring_order(n)
        self.up = [(self.order[i], self.order[(i + 1) % n]) for i in range(n)]
        self.down = [(b, a) for a, b in self.up]
        self.near = (n - 1) // 2
        self.far = n - 1 - self.near
        self.offsets = [0]
        for d in range(1, self.far + 1):
            self.offsets.append(-d)
            if d <= self.near:
                self.offsets.append(d)
        place = [0] * n
        for i, s in enumerate(self.order):
            place[s] = i
        me = lax.axis_index("seq")
        every = jnp.arange(n, dtype=jnp.int32)
        spot = jnp.sum(jnp.where(every == me, jnp.asarray(place, jnp.int32), 0))
        at = (spot + jnp.asarray(self.offsets, jnp.int32) + n) % n
        self.owners = jnp.sum(jnp.where(at[:, None] == every, jnp.asarray(self.order, jnp.int32), 0), axis=1)

    def arrange(self, x):
        pick = (self.owners[:, None] == jnp.arange(self.n)).reshape((self.n, self.n) + (1,) * (x.ndim - 1))
        return jnp.sum(jnp.where(pick, x[None], 0), axis=1)

    def hop(self, parts):
        low, high = parts[-2] if len(parts) > 1 else parts[-1], parts[-1]
        fresh = [lax.ppermute(low, "seq", self.up)]
        if len(parts) + 1 < self.n:
            fresh.append(lax.ppermute(high, "seq", self.down))
        return parts + fresh


class RingSum:
    def __init__(self, ring, last):
        self.ring, self.i, self.j = ring, ring.far, ring.near
        self.part = dict(zip(ring.offsets[-len(last) :], last))
        self.held = [self.part[-self.i], self.part[self.j]]

    def join(self, terms):
        self.part.update(zip(self.ring.offsets, terms))

    def add(self, moved, at, left):
        return (moved.astype(f32) + self.part[at].astype(f32)).astype(bf16) if left else moved

    def step(self):
        if self.j >= self.i > 0:
            self.j -= 1
            self.held[1] = self.add(lax.ppermute(self.held[1], "seq", self.ring.up), self.j, self.j)
        if self.i > 0:
            self.i -= 1
            self.held[0] = self.add(lax.ppermute(self.held[0], "seq", self.ring.down), -self.i, self.i)

    def finish(self):
        while self.i or self.j:
            self.step()
        return sum((h.astype(f32) for h in self.held), self.part[0].astype(f32))


class Halving:
    def __init__(self, rows, seq, x, early=None):
        self.rows, self.bits = rows, rows.bit_length() - 1
        self.steps = list(range(self.bits))
        self.steps.insert(self.bits if early is None else min(early, self.bits), "seq")
        self.left, self.open = self.bits, False
        self.held = [x.reshape((2,) * self.bits + (seq, -1, x.shape[-1]))]

    def settle(self, kind):
        x = self.held[0]
        if self.open:
            self.open = False
            return jnp.sum(x.astype(f32), axis=self.left).astype(kind)
        return x.astype(kind)

    def step(self):
        x, b = self.settle(bf16), self.steps.pop(0)
        if b == "seq":
            self.held, self.open = [lax.all_to_all(x, "seq", self.left, self.left)], True
            return
        self.left -= 1
        mine = (lax.axis_index("rows") >> b) & 1
        keep = lax.dynamic_index_in_dim(x, mine, self.left, keepdims=False)
        send = lax.dynamic_index_in_dim(x, 1 - mine, self.left, keepdims=False)
        got = lax.ppermute(send, "rows", [(j, j ^ (1 << b)) for j in range(self.rows)])
        self.held = [(keep.astype(f32) + got.astype(f32)).astype(bf16)]

    def finish(self):
        while self.steps:
            self.step()
        return self.settle(f32)


def slot(values, *moving):
    held = [h for m in moving for h in m.held]
    out = list(lax.optimization_barrier(tuple(values) + tuple(held)))
    for m in reversed(moving):
        m.held = out[-len(m.held) :]
        del out[-len(m.held) :]
    return out


def together(*xs):
    return lax.optimization_barrier(xs)


def norm(resid, gain, shift):
    mean = jnp.mean(resid, axis=-1, keepdims=True)
    centered = resid - mean
    inv = lax.rsqrt(jnp.mean(centered * centered, axis=-1, keepdims=True) + EPS)
    unit = centered * inv
    return unit * gain + shift, unit, inv


def norm_back(dy, unit, inv, gain):
    f = dy * gain
    mean = jnp.mean(f, axis=-1, keepdims=True)
    cross = jnp.mean(f * unit, axis=-1, keepdims=True)
    return (f - mean - unit * cross) * inv, jnp.sum(dy * unit, axis=0), jnp.sum(dy, axis=0)


def colsum(x):
    return jnp.sum(x.astype(f32), axis=0)


def key_marks(seg, hidden):
    lane = jnp.arange(128)
    marks = jnp.where(lane < 3, jnp.where(seg[..., None] == lane, 0.0, BIG), 0.0)
    if hidden is not None:
        marks = jnp.where(lane == 3, jnp.where(hidden[..., None], BIG, 0.0), marks)
    return jnp.where((lane >= 8) & (lane <= 10), 1.0, marks).astype(bf16)


def query_marks(seg):
    lane = jnp.arange(128)
    return ((seg[..., None] == lane) | (lane == 3)).astype(bf16)


def row_major(x):
    return with_layout_constraint(x, Layout(tuple(range(x.ndim))))


def layer(nrows, nseq, *args):
    (
        target, memory, target_seg, memory_seg, grad_output,
        self_query, self_qbias, self_key, self_value, self_vbias, self_out, self_obias, norm1_gain, norm1_shift,
        cross_query, cross_qbias, cross_key, cross_value, cross_vbias, cross_out, cross_obias, norm2_gain, norm2_shift,
        ffn_up, ffn_ubias, ffn_down, ffn_dbias, norm3_gain, norm3_shift,
    ) = args
    n = nrows * nseq
    R, L, D = target.shape
    c = self_query.shape[0]
    F = ffn_up.shape[1]
    m = F // D
    ring = Ring(nseq)

    mats = (self_query, self_key, self_value, self_out, cross_query, cross_key, cross_value, cross_out)
    vecs = (
        self_qbias, self_vbias, self_obias, norm1_gain, norm1_shift, cross_qbias, cross_vbias, cross_obias,
        norm2_gain, norm2_shift, ffn_dbias, norm3_gain, norm3_shift,
    )
    nvec = len(vecs)
    ids = jnp.concatenate([target_seg, memory_seg], axis=0).reshape(-1, 128)
    pack = pack_weights(mats, vecs, ffn_ubias, ids)
    everything = lax.all_gather(pack, BOTH, axis=0, tiled=True)
    x = target.reshape(R * L, D)
    parts = [row_major(x)]
    while len(parts) < nseq:
        parts = ring.hop(parts)
    pack_f = pack_ffn(ffn_up.reshape(c, n, m, c).transpose(0, 2, 1, 3).reshape(c, F), ffn_down)
    X = row_major(jnp.concatenate(parts, axis=0))
    everything, pack_f, memory, X = together(everything, pack_f, memory, X)
    wanted = ring.hop([row_major(memory.reshape(R * L, D))])
    wffn = lax.all_gather(pack_f, BOTH, axis=0, tiled=True)
    wq, wkv, wo, cq, ckv, co = [
        everything[:, a * D : b * D] for a, b in ((0, 1), (1, 3), (3, 4), (4, 5), (5, 7), (7, 8))
    ]
    vec, bu, pairs, segs = spread_lines(everything[:, 8 * D :], n, nvec, m, (1, 6), ids.shape[0])
    bq, _, bo, g1, s1, bcq, _, bco, g2, s2, bd, g3, s3 = [vec[k : k + 1] for k in range(nvec)]
    bkv, bckv = pairs[0:1], pairs[1:2]

    segs = segs.reshape(nrows, nseq, 2 * R, L)
    mine = (jnp.arange(nrows) == lax.axis_index("rows")).reshape(nrows, 1, 1, 1)
    segs = ring.arrange(jnp.sum(jnp.where(mine, segs, 0.0), axis=0).astype(jnp.int32))
    hidden = (ring.owners > lax.axis_index("seq"))[:, None, None]
    half = (nseq + 1) // 2
    self_marks = [key_marks(segs[:, :R], hidden)]
    cross_marks = [key_marks(s, None) for s in (segs[:half, R:], segs[half:, R:])]
    marks = query_marks(target_seg)

    def rows(t):
        return t.reshape(R, -1, t.shape[-1])

    def pile(parts):
        return row_major(jnp.concatenate(parts, axis=0))

    def project(parts, w, b):
        return (dot(parts, w) + b).astype(bf16).reshape(-1, R, L, 2 * D)

    def pieces(t):
        return list(t.reshape(-1, R, L, D))

    KV = [project(X, wkv, bkv)]
    Q = rows((dot(x, wq) + bq).astype(bf16))
    Q, KV[0], *wanted = together(Q, KV[0], *wanted)
    wanted = ring.hop(wanted)
    A1, lse1 = attn_fwd(Q, KV, self_marks, marks, True)
    A1, lse1, *wanted = together(A1, lse1, *wanted)
    wanted = ring.hop(wanted)
    a1 = A1.reshape(R * L, D).astype(bf16)
    R1 = x.astype(f32) + dot(a1, wo) + bo
    H1, N1, i1 = norm(R1, g1, s1)
    h1 = H1.astype(bf16)
    CQ = rows((dot(h1, cq) + bcq).astype(bf16))
    while len(wanted) < half:
        wanted = ring.hop(wanted)
    Ms = [pile(wanted[:half])]
    CKV = [project(Ms[0], ckv, bckv)]
    CQ, CKV[0], *wanted = together(CQ, CKV[0], *wanted)
    while len(wanted) < nseq:
        wanted = ring.hop(wanted)
    Ms.append(pile(wanted[half:]))
    CKV.append(project(Ms[1], ckv, bckv))
    A2, lse2 = attn_fwd(CQ, CKV, cross_marks, marks, False)
    a2 = A2.reshape(R * L, D).astype(bf16)
    R2 = H1 + dot(a2, co) + bco

    knobs = jnp.concatenate([vec[8:13], jnp.zeros((3, D), f32)], axis=0)
    output, dR2, dO2, w_ffn, dbu, sums = ffn(R2, grad_output.reshape(R * L, D), wffn, bu, knobs)
    output = rows(output)
    gbd, dg3, ds3, dg2, ds2, gbco = [sums[k : k + 1] for k in range(6)]

    def halved(w, early=None):
        return Halving(nrows, nseq, w, early)

    def scattered(w):
        return lax.psum_scatter(w, BOTH, scatter_dimension=0, tiled=True)

    npair = D // 128
    cuts = (0, npair // 3, 2 * npair // 3, npair)
    near = half * R * L
    g_ffn = scattered(w_ffn)
    w_co = dot(a2, dO2, TN).astype(bf16)
    dA2 = rows(dot(dO2, co, NT).astype(bf16))
    dA2, w_co = slot([dA2, w_co])
    dCQ, dCKV = slot(attn_bwd(CQ, CKV, cross_marks, marks, lse2, A2, dA2, False, 0, npair))
    g = dCKV.reshape(-1, 2 * D)
    dM = dot(g, ckv, NT).astype(bf16)
    dCQ = dCQ.reshape(R * L, D)
    dM, dCQ, g = slot([dM, dCQ, g])
    to_memory = RingSum(ring, pieces(dM))
    to_memory.step()
    w_ckv = (dot(Ms[0], g[:near], TN) + dot(Ms[1], g[near:], TN)).astype(bf16)
    dCQ, w_ckv = slot([dCQ, w_ckv])
    w_cq = dot(h1, dCQ, TN).astype(bf16)
    dH1 = dR2 + dot(dCQ, cq, NT)
    dR1, dg1, ds1 = norm_back(dH1, N1, i1, g1)
    dO1 = dR1.astype(bf16)
    dA1 = rows(dot(dO1, wo, NT).astype(bf16))
    w_o = dot(a1, dO1, TN).astype(bf16)
    dA1, others = slot([dA1, jnp.concatenate([w_cq, w_ckv, w_co, w_o], axis=1)], to_memory)
    to_memory.step()
    own = (Q, KV, self_marks, marks, lse1, A1, dA1, True)
    into = ()
    for k in range(3):
        if k:
            to_memory.step()
        at, count = cuts[k], cuts[k + 1] - cuts[k]
        into = attn_bwd(*own, at, count, into)
        if k == 0:
            w_kv1 = dot(X, into[1].reshape(-1, 2 * D)[:, : 256 * count], TN).astype(bf16)
            *into, w_kv1 = slot([*into, w_kv1], to_memory)
        elif k == 1:
            *into, others, g_ffn = slot([*into, others, g_ffn], to_memory)
            others = scattered(others)
        else:
            into = slot(into, to_memory)
    to_memory.step()
    dQ, dKV = into
    g = dKV.reshape(-1, 2 * D)
    dQ = dQ.reshape(R * L, D)
    dX = dot(g, wkv, NT).astype(bf16)
    g, dQ, dX = slot([g, dQ, dX])
    to_target = RingSum(ring, pieces(dX))
    to_target.step()
    w_kv2 = dot(X, g[:, 256 * cuts[1] :], TN).astype(bf16)
    (w_kv2,) = slot([w_kv2], to_target)
    to_target.step()
    w_q = dot(x, dQ, TN).astype(bf16)
    vec_sums = [
        v.reshape(1, D)
        for v in (
            colsum(dQ), colsum(dA1.reshape(R * L, D)), colsum(dO1), dg1, ds1,
            colsum(dCQ), colsum(dA2.reshape(R * L, D)), gbco, dg2, ds2, gbd, dg3, ds3,
        )
    ]
    late = jnp.concatenate([w_q, w_kv1, w_kv2, collect_lines(vec_sums, dbu, n)], axis=1)
    late = halved(late)
    late.step()
    late.step()
    to_target.step()
    late.step()
    target_gradient = (rows(dR1 + dot(dQ, wq, NT)) + rows(to_target.finish())).astype(bf16)
    memory_gradient = to_memory.finish().astype(bf16).reshape(R, L, D)
    sides = g_ffn.reshape(c, m, 2, D)
    g_up = sides[:, :, 0].reshape(c, m, n, c).transpose(0, 2, 1, 3).reshape(c, F).astype(f32)
    g_down = sides[:, :, 1].transpose(1, 0, 2).reshape(m * c, D).astype(f32)
    grads, small = finish(late.finish(), others, D, nvec, m * c, 0)
    gq, gk, gv, go, gcq, gck, gcv, gco = grads
    (gbq, gbv, gbo, gg1, gs1, gbcq, gbcv, gbco, gg2, gs2, gbd, gg3, gs3, gbu) = small
    return (
        output, target_gradient, memory_gradient,
        gq, gbq, gk, gv, gbv, go, gbo, gg1, gs1,
        gcq, gbcq, gck, gcv, gbcv, gco, gbco, gg2, gs2,
        g_up, gbu, g_down, gbd, gg3, gs3,
    )


def solution(mesh):
    act, ids, mat, vec = P("rows", "seq", None), P("rows", "seq"), P(BOTH, None), P(BOTH)
    ins = (
        act, act, ids, ids, act,
        mat, vec, mat, mat, vec, mat, vec, vec, vec,
        mat, vec, mat, mat, vec, mat, vec, vec, vec,
        mat, vec, mat, vec, vec, vec,
    )
    outs = (
        act, act, act,
        mat, vec, mat, mat, vec, mat, vec, vec, vec,
        mat, vec, mat, mat, vec, mat, vec, vec, vec,
        mat, vec, mat, vec, vec, vec,
    )
    run = functools.partial(layer, mesh.shape["rows"], mesh.shape["seq"])
    return jax.shard_map(run, mesh=mesh, in_specs=ins, out_specs=outs, check_vma=False)
```
